256 devices in a mesh: dom: 32 (over z_lo, y, core), st: 8 (over z_hi, x).
Axes of the slice: x: 4, y: 4, z: 8 (z_hi: 2, z_lo: 4; z = z_hi * 4 + z_lo), core: 2. Of those that a mesh axis runs over, the one named last changes fastest.
Arguments:
- start_states: bfloat16 [512, 114688], P('st', 'dom'), may hold values from -6 to 6
- stiffness: bfloat16 [512, 512], replicated, may hold values from -1 to 3
- cell_scale: float32 [256], P('dom'), may hold values from 0.5 to 2
- potential: float32 [114688], P('dom'), may hold values from -2 to 2
- connectivity: int32 [256, 512], P('dom'), may hold values from 0 to 3479, as said below
- shared_nodes: int32 [32, 2, 435], P('dom'), may hold values from 0 to 3479, as said below
- filter_bounds: float32 [2], replicated, may hold values from 3 to 60, as said below
Outputs:
- new_states: bfloat16 [512, 114688], P('st', 'dom')
The draws below stay inside these ranges and needn't reach their ends.
Inputs may be any that keep to these rules, and one draw needn't show every extreme that they name: `connectivity`: for each domain, its cells' entries name every one of its 3480 local nodes; nodes of a domain are numbered in a drawn order; cells of a domain share nodes as hexahedral elements of order 7 do. shared_nodes[d, 1] and shared_nodes[d + 1, 0] list the same mesh nodes in the same order; within one domain the two lists are distinct nodes and disjoint. filter_bounds[0] < filter_bounds[1].
All inputs are finite; a program needn't handle non-finite values.
Results may differ from the reference program's by a relative error of at most 0.0049.
The reference program's roundings to bfloat16 on the way count: a program that leaves them out, or rounds other values in their place, can miss the bound.
Values may be sent and summed in bfloat16 or wider, within the bound.
A program may use at most 64 MiB of HBM per device.

```python
import math
import jax
import jax.numpy as jnp
from jax import lax

ORDER = 7
NPC = 512
CB = 4
CC = 1
NS = 512
DEGREE = 3
NS_ITERS = 3
DOMS = 32
CELLS = 8
LN = 3480
LNP = 3584
SH = 435


def node_tables(key):
    base = jax.random.fold_in(key, 4242)
    per_edge = ORDER + 1
    node_across = CB * ORDER + 1
    node_depth = CC * ORDER + 1
    cell_ids = jnp.arange(CELLS)
    dof_ids = jnp.arange(NPC)
    cell_first = cell_ids // (CB * CC)
    cell_second = cell_ids // CC % CB
    cell_third = cell_ids % CC
    dof_first = dof_ids // (per_edge * per_edge)
    dof_second = dof_ids // per_edge % per_edge
    dof_third = dof_ids % per_edge
    coord_first = cell_first[:, None] * ORDER + dof_first[None, :]
    coord_second = cell_second[:, None] * ORDER + dof_second[None, :]
    coord_third = cell_third[:, None] * ORDER + dof_third[None, :]
    structured = (coord_first * node_across + coord_second) * node_depth + coord_third
    face_ids = jnp.arange(SH)
    face_row = face_ids // node_across
    face_col = face_ids % node_across
    left_face = (face_row * node_across + face_col) * node_depth
    right_face = left_face + node_depth - 1
    domain_keys = jax.random.split(base, DOMS)

    def number_domain(domain_key):
        shuffle = jax.random.permutation(domain_key, LN).astype(jnp.int32)
        return (shuffle[structured], jnp.stack([shuffle[left_face], shuffle[right_face]]))
    return jax.vmap(number_domain)(domain_keys)


def draw_connectivity(key, part):
    tables = node_tables(key)
    return tables[0].reshape(DOMS * CELLS, NPC).astype(jnp.int32)


def draw_shared_nodes(key, part):
    tables = node_tables(key)
    return tables[1].astype(jnp.int32)


def draw_stiffness(key, part):
    inner_key = jax.random.fold_in(key, 77)
    base_mat = jax.random.normal(inner_key, (NPC, NPC), jnp.float32)
    matrix = jnp.dot(base_mat, base_mat.T, precision=jax.lax.Precision.HIGHEST) / NPC
    matrix = matrix + 0.25 * jnp.eye(NPC, dtype=jnp.float32)
    return matrix.astype(jnp.bfloat16)


def draw_filter_bounds(key, part):
    first_key, second_key = jax.random.split(jax.random.fold_in(key, 91))
    bottom = jax.random.uniform(first_key, (), jnp.float32, 4.0, 8.0)
    ceiling = jax.random.uniform(second_key, (), jnp.float32, 30.0, 50.0)
    return jnp.stack([bottom, ceiling]).astype(jnp.float32)


def block_scale(key, extent, shards, low, top_value):
    def one(axis_at, shards_of):
        heights = jax.random.uniform(jax.random.fold_in(jax.random.fold_in(key, 6), axis_at), (shards_of,), jnp.float32, low / len(shards), top_value / len(shards))
        return jnp.repeat(jnp.exp(heights), extent[axis_at] // shards_of).reshape((-1,) + (1,) * (len(extent) - axis_at - 1))

    level = one(*shards[0])
    for cut in shards[1:]:
        level = level * one(*cut)
    return level


def noise(stream_key, shape, spread, most, cuts=(), kind=jnp.bfloat16):
    level = block_scale(stream_key, shape, cuts, -0.22, 0.18) if cuts else 1.0
    result = jax.random.normal(stream_key, shape, jnp.float32) * spread * level
    return jnp.minimum(jnp.maximum(result, -most), most).astype(kind)


def setup_inputs(seed: int = 0) -> dict:
    keys = jax.random.split(jax.random.key(seed), 8)
    start_states = noise(keys[0], (NS, DOMS * LNP), 1.0, 6.0, ((0, 8), (1, 32)))
    stiffness = draw_stiffness(jax.random.fold_in(keys[7], 71), 0)
    cell_scale = jnp.clip(jnp.exp(math.log(2.0) - 1.3862944 * jax.random.uniform(keys[2], (DOMS * CELLS,), jnp.float32) ** block_scale(keys[2], (DOMS * CELLS,), ((0, 32),), -0.2, 0.2)), 0.5, 2.0)
    potential = jnp.clip(jax.random.uniform(keys[3], (DOMS * LNP,), jnp.float32, -2.0, 2.0) * block_scale(keys[3], (DOMS * LNP,), ((0, 32),), -0.4, 0.0), -2.0, 2.0)
    connectivity = draw_connectivity(jax.random.fold_in(keys[7], 71), 0)
    shared_nodes = draw_shared_nodes(jax.random.fold_in(keys[7], 71), 0)
    filter_bounds = draw_filter_bounds(jax.random.fold_in(keys[7], 71), 0)
    return {"start_states": start_states, "stiffness": stiffness, "cell_scale": cell_scale, "potential": potential, "connectivity": connectivity, "shared_nodes": shared_nodes, "filter_bounds": filter_bounds}


def inverse_root(gram):
    frobenius = jnp.sqrt(jnp.sum(gram * gram) + 1e-06)
    iterate = gram / frobenius
    identity = jnp.eye(gram.shape[0], dtype=jnp.float32)
    inverse = identity
    for sweep in range(NS_ITERS):
        factor = 1.5 * identity - 0.5 * jnp.dot(inverse, iterate, precision=lax.Precision.HIGHEST)
        iterate = jnp.dot(iterate, factor, precision=lax.Precision.HIGHEST)
        inverse = jnp.dot(factor, inverse, precision=lax.Precision.HIGHEST)
    return (inverse / jnp.sqrt(frobenius)).astype(jnp.bfloat16)

def reference(start_states, stiffness, cell_scale, potential, connectivity, shared_nodes, filter_bounds):
    states = start_states.reshape(NS, DOMS, LNP).transpose(1, 0, 2)
    node_ids = jnp.arange(LNP)
    inside = (node_ids < LN).astype(jnp.bfloat16)
    states = states * inside[None, None, :]
    links_all = connectivity.reshape(DOMS, CELLS, NPC)
    scales = cell_scale.reshape(DOMS, CELLS)
    pot_all = potential.reshape(DOMS, LNP)
    stiff_wide = stiffness.astype(jnp.float32)
    left_ids = shared_nodes[:, 0]
    right_ids = shared_nodes[:, 1]

    def domain_term(items):
        block, links, scaled, pot_row = items
        values = block[:, links].astype(jnp.float32)
        products = jnp.einsum('scn,nm->scm', values, stiff_wide) * scaled[None, :, None]
        total = jnp.zeros(block.shape, jnp.float32).at[:, links.reshape(-1)].add(products.reshape(block.shape[0], -1))
        return total + pot_row[None, :] * block.astype(jnp.float32)

    def operate_all(field):
        terms = lax.map(domain_term, (field, links_all, scales, pot_all))
        right_vals = jax.vmap(lambda term, ids: term[:, ids])(terms, right_ids)
        left_vals = jax.vmap(lambda term, ids: term[:, ids])(terms, left_ids)
        zero_face = jnp.zeros_like(right_vals[:1])
        from_below = jnp.concatenate([zero_face, right_vals[:-1]], axis=0)
        from_above = jnp.concatenate([left_vals[1:], zero_face], axis=0)

        def combine(term, lower_ids, upper_ids, below, above):
            return term.at[:, lower_ids].add(below).at[:, upper_ids].add(above)
        return jax.vmap(combine)(terms, left_ids, right_ids, from_below, from_above)
    center = (filter_bounds[1] + filter_bounds[0]) / 2.0
    half_width = (filter_bounds[1] - filter_bounds[0]) / 2.0
    previous = states
    current = ((operate_all(states) - center * states.astype(jnp.float32)) / half_width).astype(jnp.bfloat16)
    for degree_step in range(DEGREE - 1):
        following = 2.0 * (operate_all(current) - center * current.astype(jnp.float32)) / half_width - previous.astype(jnp.float32)
        previous, current = (current, following.astype(jnp.bfloat16))
    domain_ids = jnp.arange(DOMS)

    def owned_mask(domain, lower_ids):
        keep = jnp.where(domain > 0, 0.0, 1.0).astype(jnp.bfloat16)
        return inside.at[lower_ids].set(keep)
    owned = jax.vmap(owned_mask)(domain_ids, left_ids)

    def accumulate(total, items):
        block, marks = items
        masked = block * marks[None, :]
        part = lax.dot_general(masked, block, (((1,), (1,)), ((), ())), preferred_element_type=jnp.float32)
        return (total + part, 0)
    gram = lax.scan(accumulate, jnp.zeros((NS, NS), jnp.float32), (current, owned))[0]
    coeffs = inverse_root(gram)

    def rotate(block):
        return lax.dot_general(coeffs, block, (((0,), (0,)), ((), ())), preferred_element_type=jnp.float32).astype(jnp.bfloat16)
    rotated = lax.map(rotate, current)
    return rotated.transpose(1, 0, 2).reshape(NS, DOMS * LNP)
```

```python
import functools
import jax
import jax.numpy as jnp
from jax import lax
from jax.experimental import pallas as pl
from jax.experimental.pallas import tpu as pltpu
from jax.sharding import PartitionSpec as P

f32 = jnp.float32
bf16 = jnp.bfloat16
DEGREE = 3
NS_ITERS = 3
CELLS = 8
NPC = 512
ENT = CELLS * NPC
LN = 3480
LNP = 3584
SH = 435
FACE = 512
SPEC = 1536
MESH_ID = pl.DeviceIdType.MESH


def one_hot_rows(row, count):
    ids = lax.broadcasted_iota(jnp.int32, (count, row.shape[1]), 0)
    return jnp.where(ids == row, 1.0, 0.0).astype(bf16)


def as_column(row):
    return jnp.transpose(jnp.broadcast_to(row, (128, 128)))


def contract_last(a, b):
    return lax.dot_general(a, b, (((1,), (1,)), ((), ())), preferred_element_type=f32)


def dot(a, b):
    return jnp.dot(a, b, preferred_element_type=f32)


def node_tables(conn, faces, oa, ob):
    total = jnp.zeros((128, 32), f32)
    seen = []
    for c in range(CELLS):
        seen.append(total)
        part = slice(c * NPC, (c + 1) * NPC)
        total = total + contract_last(oa[:, part], ob[:, part])
    place = lax.broadcasted_iota(jnp.int32, (1, FACE), 1)
    face_tabs = []
    for side in range(2):
        row = faces[side : side + 1]
        fa = one_hot_rows(lax.shift_right_arithmetic(row, 5), 128)
        fb = one_hot_rows(lax.bitwise_and(row, 31), 32)
        high = (fa * lax.shift_right_logical(place, 7).astype(f32).astype(bf16)).astype(bf16)
        low = (fa * lax.bitwise_and(place, 127).astype(f32).astype(bf16)).astype(bf16)
        face_tabs.append((contract_last(fa, fb), contract_last(high, fb), contract_last(low, fb)))
    (is_l, l_hi, l_lo), (is_r, r_hi, r_lo) = face_tabs
    other = jnp.where((total > 1.5) & (is_l + is_r < 0.5), 1.0, 0.0)
    before_b = jnp.where(
        lax.broadcasted_iota(jnp.int32, (32, 32), 0) < lax.broadcasted_iota(jnp.int32, (32, 32), 1), 1.0, 0.0
    ).astype(bf16)
    before_a = jnp.where(
        lax.broadcasted_iota(jnp.int32, (128, 128), 1) < lax.broadcasted_iota(jnp.int32, (128, 128), 0), 1.0, 0.0
    ).astype(bf16)
    row_sum = jnp.broadcast_to(jnp.sum(other, axis=1, keepdims=True), (128, 32))
    rank = dot(other.astype(bf16), before_b) + dot(before_a, row_sum.astype(bf16))
    rank = rank.astype(jnp.int32)
    slot = rank + jnp.where(rank < FACE - SH, SH, 2 * SH)
    o_hi = lax.shift_right_logical(slot, 7).astype(f32)
    o_lo = lax.bitwise_and(slot, 127).astype(f32)
    hi = jnp.where(is_l > 0.5, l_hi, jnp.where(is_r > 0.5, r_hi + FACE // 128, jnp.where(other > 0.5, o_hi, -1.0)))
    lo = jnp.where(is_l > 0.5, l_lo, jnp.where(is_r > 0.5, r_lo, jnp.where(other > 0.5, o_lo, 0.0)))
    return hi, lo, total, seen


def at_entries(tables, oa, ob):
    stacked = jnp.concatenate(tables, axis=1).astype(bf16)
    picked = lax.dot_general(stacked, oa, (((0,), (0,)), ((), ())), preferred_element_type=f32)
    wide = ob.astype(f32)
    return [
        jnp.sum(picked[32 * k : 32 * (k + 1)] * wide, axis=0, keepdims=True) for k in range(len(tables))
    ]


def split(x):
    high = x.astype(bf16)
    return high, (x - high.astype(f32)).astype(bf16)


def filter_kernel(
    doms, bounds, scale, x_ref, stiff_ref, pot_ref, conn_ref, faces_ref,
    out_ref, weight_ref, first_ref,
    oa, ob, hot, a_mat, at_mat, qa_ref, qb_ref, wpot_ref, parts, rows, sums, local, field, send, recv,
    send_sem, recv_sem,
):
    d = lax.axis_index("dom")
    has_left = d > 0
    has_right = d < doms - 1
    barrier = pltpu.get_barrier_semaphore()

    for peer in (lax.rem(d + doms - 1, doms), lax.rem(d + 1, doms)):
        pl.semaphore_signal(barrier, inc=1, device_id={"dom": peer}, device_id_type=MESH_ID)

    conn = conn_ref[...]
    faces = faces_ref[...]
    oa[...] = one_hot_rows(lax.shift_right_logical(conn, 5), 128)
    ob[...] = one_hot_rows(lax.bitwise_and(conn, 31), 32)
    hi_tab, lo_tab, count, seen = node_tables(conn, faces, oa, ob)
    pot = pot_ref[...]
    pot_hi = pot.astype(bf16).astype(f32)
    pot_mid = (pot - pot_hi).astype(bf16).astype(f32)
    pot_lo = pot - pot_hi - pot_mid
    for c in range(CELLS):
        part = slice(c * NPC, (c + 1) * NPC)
        qa, qb, cnt, p0, p1, p2, prior = at_entries(
            [hi_tab, lo_tab, count, pot_hi, pot_mid, pot_lo, seen[c]], oa[:, part], ob[:, part]
        )
        qa_ref[:, part] = qa.astype(jnp.int32)
        qb_ref[:, part] = qb.astype(jnp.int32)
        wpot_ref[:, part] = (p0 + p1 + p2) / cnt
        is_first = prior < 0.5
        on_left = (qa >= 0.0) & (qa * 128.0 + qb < SH) & has_left
        weight_ref[:, part] = jnp.where(is_first & jnp.logical_not(on_left), 1.0, 0.0)
        first_ref[:, part] = jnp.where(is_first, conn[:, part], -1)

    low_hot = one_hot_rows(lax.bitwise_and(conn, 127), 128)
    block = lax.shift_right_logical(conn, 7)
    chunk = 4
    for g in range(LNP // 128 // chunk):
        for k in range(chunk):
            mine = jnp.where(block == g * chunk + k, 1.0, 0.0).astype(bf16)
            hot[k * 128 : (k + 1) * 128] = low_hot * mine
        term = dot(x_ref[:, g * chunk * 128 : (g + 1) * chunk * 128], hot[...])
        local[...] = term if g == 0 else local[...] + term
    for c in range(CELLS):
        field[0, c * 64 : (c + 1) * 64] = local[:, c * NPC : (c + 1) * NPC].astype(bf16)

    qb_hot = one_hot_rows(qb_ref[...], 128)
    for j in range(SPEC // 128):
        mine = jnp.where(qa_ref[...] == j, 1.0, 0.0).astype(bf16)
        at_mat[j * 128 : (j + 1) * 128] = qb_hot * mine
    lane = lax.broadcasted_iota(jnp.int32, (128, 128), 1)

    @pl.loop(0, ENT // 128)
    def _(i):
        part = pl.ds(pl.multiple_of(i * 128, 128), 128)
        qa_col = as_column(qa_ref[:, part])
        qb_col = jnp.where(as_column(qb_ref[:, part]) == lane, 1.0, 0.0).astype(bf16)
        for j in range(SPEC // 128):
            mine = jnp.where(qa_col == j, 1.0, 0.0).astype(bf16)
            a_mat[part, j * 128 : (j + 1) * 128] = qb_col * mine

    pl.semaphore_wait(barrier, 2)

    center = (bounds[1] + bounds[0]) / 2.0
    half_width = (bounds[1] - bounds[0]) / 2.0
    in_face = lax.broadcasted_iota(jnp.int32, (1, FACE), 1) < SH
    for step in range(DEGREE):
        old = field.at[(step + 1) % 2]
        now = field.at[step % 2]
        products = dot(now[...], stiff_ref[...])
        for c in range(CELLS):
            part = slice(c * NPC, (c + 1) * NPC)
            block_rows = slice(c * 64, (c + 1) * 64)
            value = products[block_rows] * scale[c] + wpot_ref[:, part] * now[block_rows].astype(f32)
            local[:, part] = value
            high, low = split(value)
            parts[0:64, part] = high
            parts[64:128, part] = low
        both = dot(parts[...], a_mat[:, 0 : 2 * FACE])
        sums[:, 0 : 2 * FACE] = both[0:64] + both[64:128]
        send[step, 0] = sums[:, 0:FACE].astype(bf16)
        send[step, 1] = sums[:, FACE : 2 * FACE].astype(bf16)
        down = pltpu.make_async_remote_copy(
            src_ref=send.at[step, 0], dst_ref=recv.at[step, 1],
            send_sem=send_sem.at[step, 0], recv_sem=recv_sem.at[step, 1],
            device_id={"dom": d - 1}, device_id_type=MESH_ID)
        up = pltpu.make_async_remote_copy(
            src_ref=send.at[step, 1], dst_ref=recv.at[step, 0],
            send_sem=send_sem.at[step, 1], recv_sem=recv_sem.at[step, 0],
            device_id={"dom": d + 1}, device_id_type=MESH_ID)

        @pl.when(has_left)
        def _():
            down.start()

        @pl.when(has_right)
        def _():
            up.start()

        both = dot(parts[...], a_mat[:, 2 * FACE : SPEC])
        high, low = split(both[0:64] + both[64:128])
        rows[0:64, 2 * FACE : SPEC] = high
        rows[64:128, 2 * FACE : SPEC] = low
        spread = dot(rows[:, 2 * FACE : SPEC], at_mat[2 * FACE : SPEC])

        @pl.when(has_left)
        def _():
            down.wait_send()
            up.wait_recv()

        @pl.when(has_right)
        def _():
            up.wait_send()
            down.wait_recv()

        for side, there in ((0, has_left), (1, has_right)):
            part = slice(side * FACE, (side + 1) * FACE)
            came = jnp.where(in_face & there, recv[step, side].astype(f32), 0.0)
            high, low = split(sums[:, part] + came)
            rows[0:64, part] = high
            rows[64:128, part] = low
        spread = spread + dot(rows[:, 0 : 2 * FACE], at_mat[0 : 2 * FACE])
        spread = spread[0:64] + spread[64:128]
        for c in range(CELLS):
            part = slice(c * NPC, (c + 1) * NPC)
            block_rows = slice(c * 64, (c + 1) * 64)
            h = jnp.where(qa_ref[:, part] >= 0, spread[:, part], local[:, part])
            fresh = (h - center * now[block_rows].astype(f32)) / half_width
            if step > 0:
                fresh = 2.0 * fresh - old[block_rows].astype(f32)
            if step == DEGREE - 1:
                out_ref[block_rows] = fresh.astype(bf16)
            else:
                old[block_rows] = fresh.astype(bf16)


def filtered(start_states, stiffness, cell_scale, potential, connectivity, shared_nodes, filter_bounds, doms):
    pot_tab = jnp.pad(potential, (0, 128 * 32 - LNP)).reshape(128, 32)
    conn = connectivity.reshape(1, ENT)
    faces = jnp.pad(shared_nodes[0], ((0, 0), (0, FACE - SH)), constant_values=-1)
    vmem = pl.BlockSpec(memory_space=pltpu.VMEM)
    smem = pl.BlockSpec(memory_space=pltpu.SMEM)
    return pl.pallas_call(
        functools.partial(filter_kernel, doms),
        out_shape=(
            jax.ShapeDtypeStruct((512, NPC), bf16),
            jax.ShapeDtypeStruct((1, ENT), f32),
            jax.ShapeDtypeStruct((1, ENT), jnp.int32),
        ),
        in_specs=[smem, smem] + [vmem] * 5,
        out_specs=(vmem, vmem, vmem),
        scratch_shapes=[
            pltpu.VMEM((128, ENT), bf16),
            pltpu.VMEM((32, ENT), bf16),
            pltpu.VMEM((512, ENT), bf16),
            pltpu.VMEM((ENT, SPEC), bf16),
            pltpu.VMEM((SPEC, ENT), bf16),
            pltpu.VMEM((1, ENT), jnp.int32),
            pltpu.VMEM((1, ENT), jnp.int32),
            pltpu.VMEM((1, ENT), f32),
            pltpu.VMEM((128, ENT), bf16),
            pltpu.VMEM((128, SPEC), bf16),
            pltpu.VMEM((64, 2 * FACE), f32),
            pltpu.VMEM((64, ENT), f32),
            pltpu.VMEM((2, 512, NPC), bf16),
            pltpu.VMEM((DEGREE, 2, 64, FACE), bf16),
            pltpu.VMEM((DEGREE, 2, 64, FACE), bf16),
            pltpu.SemaphoreType.DMA((DEGREE, 2)),
            pltpu.SemaphoreType.DMA((DEGREE, 2)),
        ],
        compiler_params=pltpu.CompilerParams(
            collective_id=0, has_side_effects=True, vmem_limit_bytes=56 << 20),
        name="filter",
    )(filter_bounds, cell_scale, start_states, stiffness, pot_tab, conn, faces)


def to_nodes_kernel(x_ref, first_ref, out_ref, hot, acc):
    lane = lax.broadcasted_iota(jnp.int32, (128, 128), 1)
    for c in range(CELLS):

        @pl.loop(0, NPC // 128)
        def _(i):
            at = pl.ds(pl.multiple_of(c * NPC + i * 128, 128), 128)
            here = pl.ds(pl.multiple_of(i * 128, 128), 128)
            node = as_column(first_ref[:, at])
            low = jnp.where(lax.bitwise_and(node, 127) == lane, 1.0, 0.0).astype(bf16)
            block = lax.shift_right_arithmetic(node, 7)
            for j in range(LNP // 128):
                mine = jnp.where(block == j, 1.0, 0.0).astype(bf16)
                hot[here, j * 128 : (j + 1) * 128] = low * mine

        term = dot(x_ref[c * 64 : (c + 1) * 64], hot[...])
        acc[...] = term if c == 0 else acc[...] + term
    out_ref[...] = acc[...].astype(bf16)


def to_nodes(x, first):
    vmem = pl.BlockSpec(memory_space=pltpu.VMEM)
    return pl.pallas_call(
        to_nodes_kernel,
        out_shape=jax.ShapeDtypeStruct((64, LNP), bf16),
        in_specs=[vmem, vmem],
        out_specs=vmem,
        scratch_shapes=[pltpu.VMEM((NPC, LNP), bf16), pltpu.VMEM((64, LNP), f32)],
        compiler_params=pltpu.CompilerParams(vmem_limit_bytes=40 << 20),
        name="to_nodes",
    )(x, first)


def inverse_root(gram):
    frobenius = jnp.sqrt(jnp.sum(gram * gram) + 1e-06)
    iterate = gram / frobenius
    identity = jnp.eye(gram.shape[0], dtype=f32)
    inverse = identity
    for sweep in range(NS_ITERS):
        factor = 1.5 * identity - 0.5 * jnp.dot(inverse, iterate, precision=lax.Precision.HIGHEST)
        iterate = jnp.dot(iterate, factor, precision=lax.Precision.HIGHEST)
        inverse = jnp.dot(factor, inverse, precision=lax.Precision.HIGHEST)
    return (inverse / jnp.sqrt(frobenius)).astype(bf16)


def exchange(x):
    blocks = x.reshape(CELLS, 64, NPC)
    return lax.all_to_all(blocks, "st", split_axis=0, concat_axis=0, tiled=True).reshape(512, NPC)


def body(doms, start_states, stiffness, cell_scale, potential, connectivity, shared_nodes, filter_bounds):
    states, weight, first = filtered(
        start_states, stiffness, cell_scale, potential, connectivity, shared_nodes, filter_bounds, doms)
    mine = lax.dynamic_slice_in_dim(weight, lax.axis_index("st") * NPC, NPC, 1)
    cell = exchange(states)
    partial = contract_last((cell.astype(f32) * mine).astype(bf16), cell)
    gram = lax.psum(partial, ("dom", "st"))
    coeffs = inverse_root(gram)
    rotated = lax.dot_general(coeffs, cell, (((0,), (0,)), ((), ())), preferred_element_type=f32).astype(bf16)
    return to_nodes(exchange(rotated), first)


def solution(mesh):
    in_specs = (P("st", "dom"), P(), P("dom"), P("dom"), P("dom", None), P("dom", None, None), P())
    return jax.shard_map(
        functools.partial(body, mesh.shape["dom"]), mesh=mesh, in_specs=in_specs, out_specs=P("st", "dom"),
        check_vma=False)
```

```python
import functools
import jax
import jax.numpy as jnp
from jax import lax
from jax.experimental import pallas as pl
from jax.experimental.pallas import tpu as pltpu
from jax.sharding import PartitionSpec as P

f32 = jnp.float32
bf16 = jnp.bfloat16
DEGREE = 3
CELLS = 8
NPC = 512
ENT = CELLS * NPC
LN = 3480
LNP = 3584
SH = 435
FACE = 512
SPEC = 1536
MESH_ID = pl.DeviceIdType.MESH


def one_hot_rows(row, count):
    ids = lax.broadcasted_iota(jnp.int32, (count, row.shape[1]), 0)
    return jnp.where(ids == row, 1.0, 0.0).astype(bf16)


def as_column(row):
    return jnp.transpose(jnp.broadcast_to(row, (128, 128)))


def contract_last(a, b):
    return lax.dot_general(a, b, (((1,), (1,)), ((), ())), preferred_element_type=f32)


def dot(a, b):
    return jnp.dot(a, b, preferred_element_type=f32)


def node_tables(conn, faces, oa, ob):
    total = jnp.zeros((128, 32), f32)
    seen = []
    for c in range(CELLS):
        seen.append(total)
        part = slice(c * NPC, (c + 1) * NPC)
        total = total + contract_last(oa[:, part], ob[:, part])
    place = lax.broadcasted_iota(jnp.int32, (1, FACE), 1)
    face_tabs = []
    for side in range(2):
        row = faces[side : side + 1]
        fa = one_hot_rows(lax.shift_right_arithmetic(row, 5), 128)
        fb = one_hot_rows(lax.bitwise_and(row, 31), 32)
        high = (fa * lax.shift_right_logical(place, 7).astype(f32).astype(bf16)).astype(bf16)
        low = (fa * lax.bitwise_and(place, 127).astype(f32).astype(bf16)).astype(bf16)
        face_tabs.append((contract_last(fa, fb), contract_last(high, fb), contract_last(low, fb)))
    (is_l, l_hi, l_lo), (is_r, r_hi, r_lo) = face_tabs
    other = jnp.where((total > 1.5) & (is_l + is_r < 0.5), 1.0, 0.0)
    before_b = jnp.where(
        lax.broadcasted_iota(jnp.int32, (32, 32), 0) < lax.broadcasted_iota(jnp.int32, (32, 32), 1), 1.0, 0.0
    ).astype(bf16)
    before_a = jnp.where(
        lax.broadcasted_iota(jnp.int32, (128, 128), 1) < lax.broadcasted_iota(jnp.int32, (128, 128), 0), 1.0, 0.0
    ).astype(bf16)
    row_sum = jnp.broadcast_to(jnp.sum(other, axis=1, keepdims=True), (128, 32))
    rank = dot(other.astype(bf16), before_b) + dot(before_a, row_sum.astype(bf16))
    rank = rank.astype(jnp.int32)
    slot = rank + jnp.where(rank < FACE - SH, SH, 2 * SH)
    o_hi = lax.shift_right_logical(slot, 7).astype(f32)
    o_lo = lax.bitwise_and(slot, 127).astype(f32)
    hi = jnp.where(is_l > 0.5, l_hi, jnp.where(is_r > 0.5, r_hi + FACE // 128, jnp.where(other > 0.5, o_hi, -1.0)))
    lo = jnp.where(is_l > 0.5, l_lo, jnp.where(is_r > 0.5, r_lo, jnp.where(other > 0.5, o_lo, 0.0)))
    return hi, lo, total, seen


def at_entries(tables, oa, ob):
    stacked = jnp.concatenate(tables, axis=1).astype(bf16)
    picked = lax.dot_general(stacked, oa, (((0,), (0,)), ((), ())), preferred_element_type=f32)
    wide = ob.astype(f32)
    return [
        jnp.sum(picked[32 * k : 32 * (k + 1)] * wide, axis=0, keepdims=True) for k in range(len(tables))
    ]


def split(x):
    high = x.astype(bf16)
    return high, (x - high.astype(f32)).astype(bf16)


def filter_kernel(
    doms, bounds, scale, x_ref, stiff_ref, pot_ref, conn_ref, faces_ref,
    out_ref, weight_ref, first_ref,
    oa, ob, hot, a_mat, at_mat, qa_ref, qb_ref, wpot_ref, parts, rows, sums, local, field, send, recv,
    send_sem, recv_sem,
):
    d = lax.axis_index("dom")
    has_left = d > 0
    has_right = d < doms - 1
    barrier = pltpu.get_barrier_semaphore()

    for peer in (lax.rem(d + doms - 1, doms), lax.rem(d + 1, doms)):
        pl.semaphore_signal(barrier, inc=1, device_id={"dom": peer}, device_id_type=MESH_ID)

    conn = conn_ref[...]
    faces = faces_ref[...]
    oa[...] = one_hot_rows(lax.shift_right_logical(conn, 5), 128)
    ob[...] = one_hot_rows(lax.bitwise_and(conn, 31), 32)
    hi_tab, lo_tab, count, seen = node_tables(conn, faces, oa, ob)
    pot = pot_ref[...]
    pot_hi = pot.astype(bf16).astype(f32)
    pot_mid = (pot - pot_hi).astype(bf16).astype(f32)
    pot_lo = pot - pot_hi - pot_mid
    for c in range(CELLS):
        part = slice(c * NPC, (c + 1) * NPC)
        qa, qb, cnt, p0, p1, p2, prior = at_entries(
            [hi_tab, lo_tab, count, pot_hi, pot_mid, pot_lo, seen[c]], oa[:, part], ob[:, part]
        )
        qa_ref[:, part] = qa.astype(jnp.int32)
        qb_ref[:, part] = qb.astype(jnp.int32)
        wpot_ref[:, part] = (p0 + p1 + p2) / cnt
        is_first = prior < 0.5
        on_left = (qa >= 0.0) & (qa * 128.0 + qb < SH) & has_left
        weight_ref[:, part] = jnp.where(is_first & jnp.logical_not(on_left), 1.0, 0.0)
        first_ref[:, part] = jnp.where(is_first, conn[:, part], -1)

    low_hot = one_hot_rows(lax.bitwise_and(conn, 127), 128)
    block = lax.shift_right_logical(conn, 7)
    chunk = 4
    for g in range(LNP // 128 // chunk):
        for k in range(chunk):
            mine = jnp.where(block == g * chunk + k, 1.0, 0.0).astype(bf16)
            hot[k * 128 : (k + 1) * 128] = low_hot * mine
        term = dot(x_ref[:, g * chunk * 128 : (g + 1) * chunk * 128], hot[...])
        local[...] = term if g == 0 else local[...] + term
    for c in range(CELLS):
        field[0, c * 64 : (c + 1) * 64] = local[:, c * NPC : (c + 1) * NPC].astype(bf16)

    qb_hot = one_hot_rows(qb_ref[...], 128)
    for j in range(SPEC // 128):
        mine = jnp.where(qa_ref[...] == j, 1.0, 0.0).astype(bf16)
        at_mat[j * 128 : (j + 1) * 128] = qb_hot * mine
    lane = lax.broadcasted_iota(jnp.int32, (128, 128), 1)

    @pl.loop(0, ENT // 128)
    def _(i):
        part = pl.ds(pl.multiple_of(i * 128, 128), 128)
        qa_col = as_column(qa_ref[:, part])
        qb_col = jnp.where(as_column(qb_ref[:, part]) == lane, 1.0, 0.0).astype(bf16)
        for j in range(SPEC // 128):
            mine = jnp.where(qa_col == j, 1.0, 0.0).astype(bf16)
            a_mat[part, j * 128 : (j + 1) * 128] = qb_col * mine

    pl.semaphore_wait(barrier, 2)

    center = (bounds[1] + bounds[0]) / 2.0
    half_width = (bounds[1] - bounds[0]) / 2.0
    in_face = lax.broadcasted_iota(jnp.int32, (1, FACE), 1) < SH
    for step in range(DEGREE):
        old = field.at[(step + 1) % 2]
        now = field.at[step % 2]
        products = dot(now[...], stiff_ref[...])
        for c in range(CELLS):
            part = slice(c * NPC, (c + 1) * NPC)
            block_rows = slice(c * 64, (c + 1) * 64)
            value = products[block_rows] * scale[c] + wpot_ref[:, part] * now[block_rows].astype(f32)
            local[:, part] = value
            high, low = split(value)
            parts[0:64, part] = high
            parts[64:128, part] = low
        both = dot(parts[...], a_mat[:, 0 : 2 * FACE])
        sums[:, 0 : 2 * FACE] = both[0:64] + both[64:128]
        send[step, 0] = sums[:, 0:FACE].astype(bf16)
        send[step, 1] = sums[:, FACE : 2 * FACE].astype(bf16)
        down = pltpu.make_async_remote_copy(
            src_ref=send.at[step, 0], dst_ref=recv.at[step, 1],
            send_sem=send_sem.at[step, 0], recv_sem=recv_sem.at[step, 1],
            device_id={"dom": d - 1}, device_id_type=MESH_ID)
        up = pltpu.make_async_remote_copy(
            src_ref=send.at[step, 1], dst_ref=recv.at[step, 0],
            send_sem=send_sem.at[step, 1], recv_sem=recv_sem.at[step, 0],
            device_id={"dom": d + 1}, device_id_type=MESH_ID)

        @pl.when(has_left)
        def _():
            down.start()

        @pl.when(has_right)
        def _():
            up.start()

        both = dot(parts[...], a_mat[:, 2 * FACE : SPEC])
        high, low = split(both[0:64] + both[64:128])
        rows[0:64, 2 * FACE : SPEC] = high
        rows[64:128, 2 * FACE : SPEC] = low
        spread = dot(rows[:, 2 * FACE : SPEC], at_mat[2 * FACE : SPEC])

        @pl.when(has_left)
        def _():
            down.wait_send()
            up.wait_recv()

        @pl.when(has_right)
        def _():
            up.wait_send()
            down.wait_recv()

        for side, there in ((0, has_left), (1, has_right)):
            part = slice(side * FACE, (side + 1) * FACE)
            came = jnp.where(in_face & there, recv[step, side].astype(f32), 0.0)
            high, low = split(sums[:, part] + came)
            rows[0:64, part] = high
            rows[64:128, part] = low
        spread = spread + dot(rows[:, 0 : 2 * FACE], at_mat[0 : 2 * FACE])
        spread = spread[0:64] + spread[64:128]
        for c in range(CELLS):
            part = slice(c * NPC, (c + 1) * NPC)
            block_rows = slice(c * 64, (c + 1) * 64)
            h = jnp.where(qa_ref[:, part] >= 0, spread[:, part], local[:, part])
            fresh = (h - center * now[block_rows].astype(f32)) / half_width
            if step > 0:
                fresh = 2.0 * fresh - old[block_rows].astype(f32)
            if step == DEGREE - 1:
                out_ref[block_rows] = fresh.astype(bf16)
            else:
                old[block_rows] = fresh.astype(bf16)


def filtered(start_states, stiffness, cell_scale, potential, connectivity, shared_nodes, filter_bounds, doms):
    pot_tab = jnp.pad(potential, (0, 128 * 32 - LNP)).reshape(128, 32)
    conn = connectivity.reshape(1, ENT)
    faces = jnp.pad(shared_nodes[0], ((0, 0), (0, FACE - SH)), constant_values=-1)
    vmem = pl.BlockSpec(memory_space=pltpu.VMEM)
    smem = pl.BlockSpec(memory_space=pltpu.SMEM)
    return pl.pallas_call(
        functools.partial(filter_kernel, doms),
        out_shape=(
            jax.ShapeDtypeStruct((512, NPC), bf16),
            jax.ShapeDtypeStruct((1, ENT), f32),
            jax.ShapeDtypeStruct((1, ENT), jnp.int32),
        ),
        in_specs=[smem, smem] + [vmem] * 5,
        out_specs=(vmem, vmem, vmem),
        scratch_shapes=[
            pltpu.VMEM((128, ENT), bf16),
            pltpu.VMEM((32, ENT), bf16),
            pltpu.VMEM((512, ENT), bf16),
            pltpu.VMEM((ENT, SPEC), bf16),
            pltpu.VMEM((SPEC, ENT), bf16),
            pltpu.VMEM((1, ENT), jnp.int32),
            pltpu.VMEM((1, ENT), jnp.int32),
            pltpu.VMEM((1, ENT), f32),
            pltpu.VMEM((128, ENT), bf16),
            pltpu.VMEM((128, SPEC), bf16),
            pltpu.VMEM((64, 2 * FACE), f32),
            pltpu.VMEM((64, ENT), f32),
            pltpu.VMEM((2, 512, NPC), bf16),
            pltpu.VMEM((DEGREE, 2, 64, FACE), bf16),
            pltpu.VMEM((DEGREE, 2, 64, FACE), bf16),
            pltpu.SemaphoreType.DMA((DEGREE, 2)),
            pltpu.SemaphoreType.DMA((DEGREE, 2)),
        ],
        compiler_params=pltpu.CompilerParams(
            collective_id=0, has_side_effects=True, vmem_limit_bytes=56 << 20),
        name="filter",
    )(filter_bounds, cell_scale, start_states, stiffness, pot_tab, conn, faces)


def product(a, b):
    a_hi, a_lo = split(a)
    b_hi, b_lo = split(b)
    return dot(a_hi, b_hi) + (dot(a_hi, b_lo) + dot(a_lo, b_hi))


def finish_kernel(
    mine_ref, weight_ref, first_ref, out_ref,
    got, hot, sums, half, from_core, from_x, from_y, line, total, gram, root, turned, back, acc,
    sent, came,
):
    d = lax.axis_index("dom")
    s = lax.axis_index("st")
    core, y, z_lo = lax.rem(d, 2), lax.rem(lax.div(d, 2), 4), lax.div(d, 8)
    x, z_hi = lax.rem(s, 4), lax.div(s, 4)
    z = z_hi * 4 + z_lo

    def device(core=core, y=y, z_lo=z_lo, x=x, z_hi=z_hi):
        return {"dom": (z_lo * 4 + y) * 2 + core, "st": z_hi * 4 + x}

    def around(at, by, count):
        return lax.rem(at + by, count)

    def along_z(by):
        there = around(z, by, 8)
        return device(z_lo=lax.rem(there, 4), z_hi=lax.div(there, 4))

    count = [0]

    def copy(src, dst, to):
        k = count[0]
        count[0] += 1
        return pltpu.make_async_remote_copy(
            src_ref=src, dst_ref=dst, send_sem=sent.at[k], recv_sem=came.at[k], device_id=to, device_id_type=MESH_ID)

    def start(copies):
        for one in copies:
            one.start()
        return copies

    def finish(copies):
        for one in copies:
            one.wait()

    peers = [device(core=1 - core)]
    peers += [device(y=around(y, k, 4)) for k in range(1, 4)]
    peers += [along_z(k) for k in range(1, 8)]
    peers += [device(x=around(x, k, 4)) for k in range(1, 4)]
    peers += [device(x=around(x, k, 4), z_hi=1 - z_hi) for k in range(1, 4)]
    barrier = pltpu.get_barrier_semaphore()
    for peer in peers:
        pl.semaphore_signal(barrier, inc=1, device_id=peer, device_id_type=MESH_ID)
    pl.semaphore_wait(barrier, len(peers))

    def pair_rows(at):
        return pl.ds(pl.multiple_of(at * 128, 128), 128)

    def cell_rows(at, k):
        return pl.ds(pl.multiple_of(at * 128 + k * 64, 64), 64)

    crossing = []
    for k in range(4):
        there = around(x, k, 4)
        crossing.append(copy(
            mine_ref.at[cell_rows(there, 1 - z_hi)], got.at[s, cell_rows(0, 1 - z_hi)],
            device(x=there, z_hi=1 - z_hi)))
    start(crossing)
    beside = []
    for k in range(1, 4):
        there = around(x, k, 4)
        beside.append(copy(mine_ref.at[pair_rows(there)], got.at[s], device(x=there)))
    start(beside)
    late = []
    for k in range(4):
        there = around(x, k, 4)
        late.append(copy(
            mine_ref.at[cell_rows(there, z_hi)], got.at[s, cell_rows(0, z_hi)],
            device(x=there, z_hi=1 - z_hi)))
    start(late)
    got[s] = mine_ref[pair_rows(x)]

    lane = lax.broadcasted_iota(jnp.int32, (128, 128), 1)

    @pl.loop(0, ENT // 128)
    def _(i):
        at = pl.ds(pl.multiple_of(i * 128, 128), 128)
        node = as_column(first_ref[:, at])
        low = jnp.where(lax.bitwise_and(node, 127) == lane, 1.0, 0.0).astype(bf16)
        block = lax.shift_right_arithmetic(node, 7)
        for j in range(LNP // 128):
            mine = jnp.where(block == j, 1.0, 0.0).astype(bf16)
            hot[at, j * 128 : (j + 1) * 128] = low * mine

    finish(beside)
    finish(crossing)

    def weighted(rows, at):
        mark = weight_ref[:, pl.ds(pl.multiple_of(at * NPC, NPC), NPC)]
        return (rows.astype(f32) * mark).astype(bf16)

    own = pl.ds(pl.multiple_of(z_hi * 4, 4), 4)
    first_cell = got[own, 0:64].reshape(256, NPC)
    second_cell = got[own, 64:128].reshape(256, NPC)
    sums[0] = contract_last(weighted(first_cell, 2 * x), first_cell) + contract_last(
        weighted(second_cell, 2 * x + 1), second_cell)
    shared_rows = pl.ds(pl.multiple_of(z_hi * 64, 64), 64)
    low_half = got[0:4, shared_rows].reshape(256, NPC)
    high_half = got[4:8, shared_rows].reshape(256, NPC)
    sums[1] = contract_last(weighted(low_half, 2 * x + z_hi), high_half)

    half[0] = sums[0].astype(bf16)
    half[1] = sums[1].astype(bf16)
    finish(start([copy(half.at[1 - core], from_core, device(core=1 - core))]))
    sums[core] = sums[core] + from_core[...].astype(f32)
    half[core] = sums[core].astype(bf16)
    finish(start([
        copy(half.at[core, pl.ds(pl.multiple_of(around(x, k, 4) * 64, 64), 64)], from_x.at[k - 1],
             device(x=around(x, k, 4)))
        for k in range(1, 4)]))
    quarter = sums[core, pl.ds(pl.multiple_of(x * 64, 64), 64)]
    for k in range(3):
        quarter = quarter + from_x[k].astype(f32)
    sums[0, 0:64] = quarter
    turned[0, 0:64, 0:256] = quarter.astype(bf16)
    finish(start([
        copy(turned.at[0, pl.ds(pl.multiple_of(around(y, k, 4) * 16, 16), 16), pl.ds(0, 256)], from_y.at[k - 1],
             device(y=around(y, k, 4)))
        for k in range(1, 4)]))
    piece = sums[0, pl.ds(pl.multiple_of(y * 16, 16), 16)]
    for k in range(3):
        piece = piece + from_y[k].astype(f32)
    line[z] = piece.astype(bf16)
    finish(start([copy(line.at[z], line.at[z], along_z(k)) for k in range(1, 8)]))
    low_sum = line[0].astype(f32)
    high_sum = line[4].astype(f32)
    for k in range(1, 4):
        low_sum = low_sum + line[k].astype(f32)
        high_sum = high_sum + line[4 + k].astype(f32)
    on_core = 2 * core
    piece_rows = pl.ds(pl.multiple_of(x * 64 + y * 16, 16), 16)

    @pl.when(core == 0)
    def _():
        total[1, piece_rows] = high_sum.astype(bf16)

    total[on_core, piece_rows] = (low_sum + jnp.where(core == 1, high_sum, 0.0)).astype(bf16)

    def spread(rows, to):
        first = [copy(total.at[on_core, rows], total.at[on_core, rows], one) for one in to]
        second = [copy(total.at[1, rows], total.at[1, rows], one) for one in to]
        start(first)

        @pl.when(core == 0)
        def _():
            start(second)

        finish(first)

        @pl.when(core == 0)
        def _():
            finish(second)

    spread(piece_rows, [device(y=around(y, k, 4)) for k in range(1, 4)])
    spread(pl.ds(pl.multiple_of(x * 64, 64), 64), [device(x=around(x, k, 4)) for k in range(1, 4)])
    down = [copy(total.at[k], total.at[k], device(core=1 - core)) for k in range(3)]

    @pl.when(core == 0)
    def _():
        start(down[0:2])
        for one in down[0:2]:
            one.wait_send()
        down[2].wait_recv()

    @pl.when(core == 1)
    def _():
        start(down[2:3])
        down[2].wait_send()
        for one in down[0:2]:
            one.wait_recv()

    upper = total[2].astype(f32)
    gram[0:256, 0:256] = total[0].astype(f32)
    gram[256:512, 256:512] = total[1].astype(f32)
    gram[0:256, 256:512] = upper
    gram[256:512, 0:256] = jnp.transpose(upper)
    g = gram[...]
    frobenius = jnp.sqrt(jnp.sum(jnp.sum(g * g, axis=1, keepdims=True), axis=0, keepdims=True) + 1e-06)
    a = g / frobenius
    gram[...] = a
    square = product(a, a)
    diagonal = lax.broadcasted_iota(jnp.int32, (512, 512), 0) == lax.broadcasted_iota(jnp.int32, (512, 512), 1)
    root[...] = (
        jnp.where(diagonal, 2.25, 0.0) - 2.4375 * a + 1.6875 * square
        + product(square, 0.0625 * square - 0.5625 * a))
    columns = root[:, pl.ds(pl.multiple_of(z_hi * 256, 256), 256)]
    cubed = product(root[...], product(root[...], columns))
    coeffs = ((1.5 * columns - 0.5 * product(gram[...], cubed)) / jnp.sqrt(frobenius)).astype(bf16)

    finish(late)
    for k in range(2):
        cell = got[:, k * 64 : (k + 1) * 64].reshape(512, NPC)
        rotated = lax.dot_general(coeffs, cell, (((0,), (0,)), ((), ())), preferred_element_type=f32)
        turned[:, k * 64 : (k + 1) * 64] = rotated.astype(bf16).reshape(4, 64, NPC)
    returned = start([
        copy(turned.at[around(x, k, 4)], back.at[x], device(x=around(x, k, 4))) for k in range(1, 4)])
    back[x] = turned[x]
    for k in range(4):
        source = around(x, 4 - k, 4)
        if k:
            returned[k - 1].wait()
        pair = jnp.concatenate([back[source, 0:64], back[source, 64:128]], axis=1)
        term = dot(pair, hot[pl.ds(pl.multiple_of(source * 1024, 1024), 1024)])
        if k == 0:
            acc[...] = term
        elif k < 3:
            acc[...] = acc[...] + term
        else:
            out_ref[...] = (acc[...] + term).astype(bf16)


def finished(states, weight, first):
    vmem = pl.BlockSpec(memory_space=pltpu.VMEM)
    copies = 11 + 1 + 3 + 3 + 7 + 12 + 3 + 3
    return pl.pallas_call(
        finish_kernel,
        out_shape=jax.ShapeDtypeStruct((64, LNP), bf16),
        in_specs=[vmem] * 3,
        out_specs=vmem,
        scratch_shapes=[
            pltpu.VMEM((8, 128, NPC), bf16),
            pltpu.VMEM((ENT, LNP), bf16),
            pltpu.VMEM((2, 256, 256), f32),
            pltpu.VMEM((2, 256, 256), bf16),
            pltpu.VMEM((256, 256), bf16),
            pltpu.VMEM((3, 64, 256), bf16),
            pltpu.VMEM((3, 16, 256), bf16),
            pltpu.VMEM((8, 16, 256), bf16),
            pltpu.VMEM((3, 256, 256), bf16),
            pltpu.VMEM((512, 512), f32),
            pltpu.VMEM((512, 512), f32),
            pltpu.VMEM((4, 128, NPC), bf16),
            pltpu.VMEM((4, 128, NPC), bf16),
            pltpu.VMEM((64, LNP), f32),
            pltpu.SemaphoreType.DMA((copies,)),
            pltpu.SemaphoreType.DMA((copies,)),
        ],
        compiler_params=pltpu.CompilerParams(
            collective_id=1, has_side_effects=True, vmem_limit_bytes=56 << 20),
        name="finish",
    )(states, weight, first)


def body(doms, start_states, stiffness, cell_scale, potential, connectivity, shared_nodes, filter_bounds):
    states, weight, first = filtered(
        start_states, stiffness, cell_scale, potential, connectivity, shared_nodes, filter_bounds, doms)
    return finished(states, weight, first)


def solution(mesh):
    in_specs = (P("st", "dom"), P(), P("dom"), P("dom"), P("dom", None), P("dom", None, None), P())
    return jax.shard_map(
        functools.partial(body, mesh.shape["dom"]), mesh=mesh, in_specs=in_specs, out_specs=P("st", "dom"),
        check_vma=False)
```

```python
import functools
import jax
import jax.numpy as jnp
from jax import lax
from jax.experimental import pallas as pl
from jax.experimental.pallas import tpu as pltpu
from jax.sharding import PartitionSpec as P

f32 = jnp.float32
bf16 = jnp.bfloat16
DEGREE = 3
CELLS = 8
NPC = 512
ENT = CELLS * NPC
LN = 3480
LNP = 3584
SH = 435
FACE = 512
SPEC = 1536
MESH_ID = pl.DeviceIdType.MESH


def one_hot_rows(row, count):
    ids = lax.broadcasted_iota(jnp.int32, (count, row.shape[1]), 0)
    return jnp.where(ids == row, 1.0, 0.0).astype(bf16)


def as_column(row):
    return jnp.transpose(jnp.broadcast_to(row, (128, 128)))


def contract_last(a, b):
    return lax.dot_general(a, b, (((1,), (1,)), ((), ())), preferred_element_type=f32)


def dot(a, b):
    return jnp.dot(a, b, preferred_element_type=f32)


def node_tables(faces, oa, ob):
    total = jnp.zeros((128, 32), f32)
    seen = []
    for c in range(CELLS):
        seen.append(total)
        part = slice(c * NPC, (c + 1) * NPC)
        total = total + contract_last(oa[:, part], ob[:, part])
    place = lax.broadcasted_iota(jnp.int32, (1, FACE), 1)
    face_tabs = []
    for side in range(2):
        row = faces[side : side + 1]
        fa = one_hot_rows(lax.shift_right_arithmetic(row, 5), 128)
        fb = one_hot_rows(lax.bitwise_and(row, 31), 32)
        high = (fa * lax.shift_right_logical(place, 7).astype(f32).astype(bf16)).astype(bf16)
        low = (fa * lax.bitwise_and(place, 127).astype(f32).astype(bf16)).astype(bf16)
        face_tabs.append((contract_last(fa, fb), contract_last(high, fb), contract_last(low, fb)))
    (is_l, l_hi, l_lo), (is_r, r_hi, r_lo) = face_tabs
    other = jnp.where((total > 1.5) & (is_l + is_r < 0.5), 1.0, 0.0)
    before_b = jnp.where(
        lax.broadcasted_iota(jnp.int32, (32, 32), 0) < lax.broadcasted_iota(jnp.int32, (32, 32), 1), 1.0, 0.0
    ).astype(bf16)
    before_a = jnp.where(
        lax.broadcasted_iota(jnp.int32, (128, 128), 1) < lax.broadcasted_iota(jnp.int32, (128, 128), 0), 1.0, 0.0
    ).astype(bf16)
    row_sum = jnp.broadcast_to(jnp.sum(other, axis=1, keepdims=True), (128, 32))
    rank = dot(other.astype(bf16), before_b) + dot(before_a, row_sum.astype(bf16))
    rank = rank.astype(jnp.int32)
    slot = rank + jnp.where(rank < FACE - SH, SH, 2 * SH)
    o_hi = lax.shift_right_logical(slot, 7).astype(f32)
    o_lo = lax.bitwise_and(slot, 127).astype(f32)
    hi = jnp.where(is_l > 0.5, l_hi, jnp.where(is_r > 0.5, r_hi + FACE // 128, jnp.where(other > 0.5, o_hi, -1.0)))
    lo = jnp.where(is_l > 0.5, l_lo, jnp.where(is_r > 0.5, r_lo, jnp.where(other > 0.5, o_lo, 0.0)))
    return hi, lo, total, seen


def at_entries(tables, oa, ob):
    stacked = jnp.concatenate(tables, axis=1).astype(bf16)
    picked = lax.dot_general(stacked, oa, (((0,), (0,)), ((), ())), preferred_element_type=f32)
    wide = ob.astype(f32)
    return [
        jnp.sum(picked[32 * k : 32 * (k + 1)] * wide, axis=0, keepdims=True) for k in range(len(tables))
    ]


def split(x):
    high = x.astype(bf16)
    return high, (x - high.astype(f32)).astype(bf16)


def filter_kernel(
    doms, bounds, scale, x_ref, stiff_ref, pot_ref, conn_ref, faces_ref,
    out_ref, weight_ref, first_ref,
    nodes, faces, pot_rows, pot_tab, oa, ob, hot, a_mat, at_mat, qa_ref, qb_ref, wpot_ref, parts, rows, sums, local, field, send, recv,
    send_sem, recv_sem,
):
    d = lax.axis_index("dom")
    has_left = d > 0
    has_right = d < doms - 1
    barrier = pltpu.get_barrier_semaphore()

    for peer in (lax.rem(d + doms - 1, doms), lax.rem(d + 1, doms)):
        pl.semaphore_signal(barrier, inc=1, device_id={"dom": peer}, device_id_type=MESH_ID)

    for c in range(CELLS):
        nodes[:, c * NPC : (c + 1) * NPC] = conn_ref[c : c + 1]
    faces[...] = jnp.full((2, FACE), -1, jnp.int32)
    faces[:, 0:SH] = faces_ref[0]
    pot_rows[...] = jnp.zeros((32, 128), f32)
    for k in range(LNP // 128):
        pot_rows[k : k + 1] = pot_ref[pl.ds(k * 128, 128)].reshape(1, 128)
    for k in range(4):
        pot_tab[pl.ds(k, 32, stride=4)] = pot_rows[:, k * 32 : (k + 1) * 32]
    conn = nodes[...]
    oa[...] = one_hot_rows(lax.shift_right_logical(conn, 5), 128)
    ob[...] = one_hot_rows(lax.bitwise_and(conn, 31), 32)
    hi_tab, lo_tab, count, seen = node_tables(faces[...], oa, ob)
    pot = pot_tab[...]
    pot_hi = pot.astype(bf16).astype(f32)
    pot_mid = (pot - pot_hi).astype(bf16).astype(f32)
    pot_lo = pot - pot_hi - pot_mid
    for c in range(CELLS):
        part = slice(c * NPC, (c + 1) * NPC)
        qa, qb, cnt, p0, p1, p2, prior = at_entries(
            [hi_tab, lo_tab, count, pot_hi, pot_mid, pot_lo, seen[c]], oa[:, part], ob[:, part]
        )
        qa_ref[:, part] = qa.astype(jnp.int32)
        qb_ref[:, part] = qb.astype(jnp.int32)
        wpot_ref[:, part] = (p0 + p1 + p2) / cnt
        is_first = prior < 0.5
        on_left = (qa >= 0.0) & (qa * 128.0 + qb < SH) & has_left
        weight_ref[:, part] = jnp.where(is_first & jnp.logical_not(on_left), 1.0, 0.0)
        first_ref[:, part] = jnp.where(is_first, conn[:, part], -1)

    low_hot = one_hot_rows(lax.bitwise_and(conn, 127), 128)
    block = lax.shift_right_logical(conn, 7)
    chunk = 4
    for g in range(LNP // 128 // chunk):
        for k in range(chunk):
            mine = jnp.where(block == g * chunk + k, 1.0, 0.0).astype(bf16)
            hot[k * 128 : (k + 1) * 128] = low_hot * mine
        term = dot(x_ref[:, g * chunk * 128 : (g + 1) * chunk * 128], hot[...])
        local[...] = term if g == 0 else local[...] + term
    for c in range(CELLS):
        field[0, c * 64 : (c + 1) * 64] = local[:, c * NPC : (c + 1) * NPC].astype(bf16)

    qb_hot = one_hot_rows(qb_ref[...], 128)
    for j in range(SPEC // 128):
        mine = jnp.where(qa_ref[...] == j, 1.0, 0.0).astype(bf16)
        at_mat[j * 128 : (j + 1) * 128] = qb_hot * mine
    lane = lax.broadcasted_iota(jnp.int32, (128, 128), 1)

    @pl.loop(0, ENT // 128)
    def _(i):
        part = pl.ds(pl.multiple_of(i * 128, 128), 128)
        qa_col = as_column(qa_ref[:, part])
        qb_col = jnp.where(as_column(qb_ref[:, part]) == lane, 1.0, 0.0).astype(bf16)
        for j in range(SPEC // 128):
            mine = jnp.where(qa_col == j, 1.0, 0.0).astype(bf16)
            a_mat[part, j * 128 : (j + 1) * 128] = qb_col * mine

    pl.semaphore_wait(barrier, 2)

    center = (bounds[1] + bounds[0]) / 2.0
    half_width = (bounds[1] - bounds[0]) / 2.0
    in_face = lax.broadcasted_iota(jnp.int32, (1, FACE), 1) < SH
    for step in range(DEGREE):
        old = field.at[(step + 1) % 2]
        now = field.at[step % 2]
        products = dot(now[...], stiff_ref[...])
        for c in range(CELLS):
            part = slice(c * NPC, (c + 1) * NPC)
            block_rows = slice(c * 64, (c + 1) * 64)
            value = products[block_rows] * scale[c] + wpot_ref[:, part] * now[block_rows].astype(f32)
            local[:, part] = value
            high, low = split(value)
            parts[0:64, part] = high
            parts[64:128, part] = low
        both = dot(parts[...], a_mat[:, 0 : 2 * FACE])
        sums[:, 0 : 2 * FACE] = both[0:64] + both[64:128]
        send[step, 0] = sums[:, 0:FACE].astype(bf16)
        send[step, 1] = sums[:, FACE : 2 * FACE].astype(bf16)
        down = pltpu.make_async_remote_copy(
            src_ref=send.at[step, 0], dst_ref=recv.at[step, 1],
            send_sem=send_sem.at[step, 0], recv_sem=recv_sem.at[step, 1],
            device_id={"dom": d - 1}, device_id_type=MESH_ID)
        up = pltpu.make_async_remote_copy(
            src_ref=send.at[step, 1], dst_ref=recv.at[step, 0],
            send_sem=send_sem.at[step, 1], recv_sem=recv_sem.at[step, 0],
            device_id={"dom": d + 1}, device_id_type=MESH_ID)

        @pl.when(has_left)
        def _():
            down.start()

        @pl.when(has_right)
        def _():
            up.start()

        both = dot(parts[...], a_mat[:, 2 * FACE : SPEC])
        high, low = split(both[0:64] + both[64:128])
        rows[0:64, 2 * FACE : SPEC] = high
        rows[64:128, 2 * FACE : SPEC] = low
        spread = dot(rows[:, 2 * FACE : SPEC], at_mat[2 * FACE : SPEC])

        @pl.when(has_left)
        def _():
            down.wait_send()
            up.wait_recv()

        @pl.when(has_right)
        def _():
            up.wait_send()
            down.wait_recv()

        for side, there in ((0, has_left), (1, has_right)):
            part = slice(side * FACE, (side + 1) * FACE)
            came = jnp.where(in_face & there, recv[step, side].astype(f32), 0.0)
            high, low = split(sums[:, part] + came)
            rows[0:64, part] = high
            rows[64:128, part] = low
        spread = spread + dot(rows[:, 0 : 2 * FACE], at_mat[0 : 2 * FACE])
        spread = spread[0:64] + spread[64:128]
        for c in range(CELLS):
            part = slice(c * NPC, (c + 1) * NPC)
            block_rows = slice(c * 64, (c + 1) * 64)
            h = jnp.where(qa_ref[:, part] >= 0, spread[:, part], local[:, part])
            fresh = (h - center * now[block_rows].astype(f32)) / half_width
            if step > 0:
                fresh = 2.0 * fresh - old[block_rows].astype(f32)
            if step == DEGREE - 1:
                out_ref[block_rows] = fresh.astype(bf16)
            else:
                old[block_rows] = fresh.astype(bf16)


def filtered(start_states, stiffness, cell_scale, potential, connectivity, shared_nodes, filter_bounds, doms):
    vmem = pl.BlockSpec(memory_space=pltpu.VMEM)
    smem = pl.BlockSpec(memory_space=pltpu.SMEM)
    return pl.pallas_call(
        functools.partial(filter_kernel, doms),
        out_shape=(
            jax.ShapeDtypeStruct((512, NPC), bf16),
            jax.ShapeDtypeStruct((1, ENT), f32),
            jax.ShapeDtypeStruct((1, ENT), jnp.int32),
        ),
        in_specs=[smem, smem] + [vmem] * 5,
        out_specs=(vmem, vmem, vmem),
        scratch_shapes=[
            pltpu.VMEM((1, ENT), jnp.int32),
            pltpu.VMEM((2, FACE), jnp.int32),
            pltpu.VMEM((32, 128), f32),
            pltpu.VMEM((128, 32), f32),
            pltpu.VMEM((128, ENT), bf16),
            pltpu.VMEM((32, ENT), bf16),
            pltpu.VMEM((512, ENT), bf16),
            pltpu.VMEM((ENT, SPEC), bf16),
            pltpu.VMEM((SPEC, ENT), bf16),
            pltpu.VMEM((1, ENT), jnp.int32),
            pltpu.VMEM((1, ENT), jnp.int32),
            pltpu.VMEM((1, ENT), f32),
            pltpu.VMEM((128, ENT), bf16),
            pltpu.VMEM((128, SPEC), bf16),
            pltpu.VMEM((64, 2 * FACE), f32),
            pltpu.VMEM((64, ENT), f32),
            pltpu.VMEM((2, 512, NPC), bf16),
            pltpu.VMEM((DEGREE, 2, 64, FACE), bf16),
            pltpu.VMEM((DEGREE, 2, 64, FACE), bf16),
            pltpu.SemaphoreType.DMA((DEGREE, 2)),
            pltpu.SemaphoreType.DMA((DEGREE, 2)),
        ],
        compiler_params=pltpu.CompilerParams(
            collective_id=0, has_side_effects=True, vmem_limit_bytes=56 << 20),
        name="filter",
    )(filter_bounds, cell_scale, start_states, stiffness, potential, connectivity, shared_nodes)


def product(a, b):
    a_hi, a_lo = split(a)
    b_hi, b_lo = split(b)
    return dot(a_hi, b_hi) + (dot(a_hi, b_lo) + dot(a_lo, b_hi))


def finish_kernel(
    mine_ref, weight_ref, first_ref, out_ref,
    got, hot, sums, half, from_core, from_plane, line, total, gram, root, turned, back, acc,
    sent, came,
):
    d = lax.axis_index("dom")
    s = lax.axis_index("st")
    core, y, z_lo = lax.rem(d, 2), lax.rem(lax.div(d, 2), 4), lax.div(d, 8)
    x, z_hi = lax.rem(s, 4), lax.div(s, 4)
    z = z_hi * 4 + z_lo

    def device(core=core, y=y, z_lo=z_lo, x=x, z_hi=z_hi):
        return {"dom": (z_lo * 4 + y) * 2 + core, "st": z_hi * 4 + x}

    def around(at, by, count):
        return lax.rem(at + by, count)

    def along_z(by):
        there = around(z, by, 8)
        return device(z_lo=lax.rem(there, 4), z_hi=lax.div(there, 4))

    count = [0]

    def copy(src, dst, to):
        k = count[0]
        count[0] += 1
        return pltpu.make_async_remote_copy(
            src_ref=src, dst_ref=dst, send_sem=sent.at[k], recv_sem=came.at[k], device_id=to, device_id_type=MESH_ID)

    def start(copies):
        for one in copies:
            one.start()
        return copies

    def finish(copies):
        for one in copies:
            one.wait()

    peers = [device(core=1 - core)]
    peers += [
        device(x=around(x, kx, 4), y=around(y, ky, 4)) for kx in range(4) for ky in range(4) if kx + ky]
    peers += [along_z(k) for k in range(1, 8)]
    peers += [device(x=around(x, k, 4), z_hi=1 - z_hi) for k in range(1, 4)]
    barrier = pltpu.get_barrier_semaphore()
    for peer in peers:
        pl.semaphore_signal(barrier, inc=1, device_id=peer, device_id_type=MESH_ID)
    pl.semaphore_wait(barrier, len(peers))

    def pair_rows(at):
        return pl.ds(pl.multiple_of(at * 128, 128), 128)

    def cell_rows(at, k):
        return pl.ds(pl.multiple_of(at * 128 + k * 64, 64), 64)

    crossing = []
    for k in range(4):
        there = around(x, k, 4)
        crossing.append(copy(
            mine_ref.at[cell_rows(there, 1 - z_hi)], got.at[s, cell_rows(0, 1 - z_hi)],
            device(x=there, z_hi=1 - z_hi)))
    start(crossing)
    beside = []
    for k in range(1, 4):
        there = around(x, k, 4)
        beside.append(copy(mine_ref.at[pair_rows(there)], got.at[s], device(x=there)))
    start(beside)
    late = []
    for k in range(4):
        there = around(x, k, 4)
        late.append(copy(
            mine_ref.at[cell_rows(there, z_hi)], got.at[s, cell_rows(0, z_hi)],
            device(x=there, z_hi=1 - z_hi)))
    got[s] = mine_ref[pair_rows(x)]

    lane = lax.broadcasted_iota(jnp.int32, (128, 128), 1)

    @pl.loop(0, ENT // 128)
    def _(i):
        at = pl.ds(pl.multiple_of(i * 128, 128), 128)
        node = as_column(first_ref[:, at])
        low = jnp.where(lax.bitwise_and(node, 127) == lane, 1.0, 0.0).astype(bf16)
        block = lax.shift_right_arithmetic(node, 7)
        for j in range(LNP // 128):
            mine = jnp.where(block == j, 1.0, 0.0).astype(bf16)
            hot[at, j * 128 : (j + 1) * 128] = low * mine

    finish(crossing)
    start(late[0:2])
    finish(beside)

    def weighted(rows, at):
        mark = weight_ref[:, pl.ds(pl.multiple_of(at * NPC, NPC), NPC)]
        return (rows.astype(f32) * mark).astype(bf16)

    own = pl.ds(pl.multiple_of(z_hi * 4, 4), 4)
    first_cell = got[own, 0:64].reshape(256, NPC)
    second_cell = got[own, 64:128].reshape(256, NPC)
    sums[0] = contract_last(weighted(first_cell, 2 * x), first_cell) + contract_last(
        weighted(second_cell, 2 * x + 1), second_cell)
    shared_rows = pl.ds(pl.multiple_of(z_hi * 64, 64), 64)
    low_half = got[0:4, shared_rows].reshape(256, NPC)
    high_half = got[4:8, shared_rows].reshape(256, NPC)
    sums[1] = contract_last(weighted(low_half, 2 * x + z_hi), high_half)

    half[0] = sums[0].astype(bf16)
    half[1] = sums[1].astype(bf16)
    finish(start([copy(half.at[1 - core], from_core, device(core=1 - core))]))
    sums[core] = sums[core] + from_core[...].astype(f32)
    half[core] = sums[core].astype(bf16)
    plane = [(kx, ky) for kx in range(4) for ky in range(4)][1:]

    def piece_of(kx, ky):
        return pl.ds(pl.multiple_of(around(x, kx, 4) * 64 + around(y, ky, 4) * 16, 16), 16)

    def in_plane(kx, ky):
        return device(x=around(x, kx, 4), y=around(y, ky, 4))

    finish(start([
        copy(half.at[core, piece_of(*by)], from_plane.at[k], in_plane(*by)) for k, by in enumerate(plane)]))
    piece = sums[core, piece_of(0, 0)]
    for k in range(15):
        piece = piece + from_plane[k].astype(f32)
    line[z] = piece.astype(bf16)
    finish(start([copy(line.at[z], line.at[z], along_z(k)) for k in range(1, 8)]))
    start(late[2:4])
    low_sum = line[0].astype(f32)
    high_sum = line[4].astype(f32)
    for k in range(1, 4):
        low_sum = low_sum + line[k].astype(f32)
        high_sum = high_sum + line[4 + k].astype(f32)
    on_core = 2 * core
    piece_rows = piece_of(0, 0)

    @pl.when(core == 0)
    def _():
        total[1, piece_rows] = high_sum.astype(bf16)

    total[on_core, piece_rows] = (low_sum + jnp.where(core == 1, high_sum, 0.0)).astype(bf16)
    held = [copy(total.at[pl.ds(0, 2), piece_rows], total.at[pl.ds(0, 2), piece_rows], in_plane(*by)) for by in plane]
    count[0] -= len(plane)
    held_one = [copy(total.at[2, piece_rows], total.at[2, piece_rows], in_plane(*by)) for by in plane]

    @pl.when(core == 0)
    def _():
        finish(start(held))

    @pl.when(core == 1)
    def _():
        finish(start(held_one))

    down = [copy(total.at[k], total.at[k], device(core=1 - core)) for k in range(3)]

    @pl.when(core == 0)
    def _():
        start(down[0:2])
        for one in down[0:2]:
            one.wait_send()
        down[2].wait_recv()

    @pl.when(core == 1)
    def _():
        start(down[2:3])
        down[2].wait_send()
        for one in down[0:2]:
            one.wait_recv()

    upper = total[2].astype(f32)
    gram[0:256, 0:256] = total[0].astype(f32)
    gram[256:512, 256:512] = total[1].astype(f32)
    gram[0:256, 256:512] = upper
    gram[256:512, 0:256] = jnp.transpose(upper)
    g = gram[...]
    frobenius = jnp.sqrt(jnp.sum(jnp.sum(g * g, axis=1, keepdims=True), axis=0, keepdims=True) + 1e-06)
    a = g / frobenius
    gram[...] = a
    square = product(a, a)
    diagonal = lax.broadcasted_iota(jnp.int32, (512, 512), 0) == lax.broadcasted_iota(jnp.int32, (512, 512), 1)
    root[...] = (
        jnp.where(diagonal, 2.25, 0.0) - 2.4375 * a + 1.6875 * square
        + product(square, 0.0625 * square - 0.5625 * a))
    columns = root[:, pl.ds(pl.multiple_of(z_hi * 256, 256), 256)]
    cubed = product(root[...], product(root[...], columns))
    coeffs = ((1.5 * columns - 0.5 * product(gram[...], cubed)) / jnp.sqrt(frobenius)).astype(bf16)

    finish(late)
    for k in range(2):
        cell = got[:, k * 64 : (k + 1) * 64].reshape(512, NPC)
        rotated = lax.dot_general(coeffs, cell, (((0,), (0,)), ((), ())), preferred_element_type=f32)
        turned[:, k * 64 : (k + 1) * 64] = rotated.astype(bf16).reshape(4, 64, NPC)
    returned = start([
        copy(turned.at[around(x, k, 4)], back.at[x], device(x=around(x, k, 4))) for k in range(1, 4)])
    back[x] = turned[x]
    for k in range(4):
        source = around(x, 4 - k, 4)
        if k:
            returned[k - 1].wait()
        pair = jnp.concatenate([back[source, 0:64], back[source, 64:128]], axis=1)
        term = dot(pair, hot[pl.ds(pl.multiple_of(source * 1024, 1024), 1024)])
        if k == 0:
            acc[...] = term
        elif k < 3:
            acc[...] = acc[...] + term
        else:
            out_ref[...] = (acc[...] + term).astype(bf16)


def finished(states, weight, first):
    vmem = pl.BlockSpec(memory_space=pltpu.VMEM)
    copies = 11 + 1 + 15 + 7 + 15 + 3 + 3
    return pl.pallas_call(
        finish_kernel,
        out_shape=jax.ShapeDtypeStruct((64, LNP), bf16),
        in_specs=[vmem] * 3,
        out_specs=vmem,
        scratch_shapes=[
            pltpu.VMEM((8, 128, NPC), bf16),
            pltpu.VMEM((ENT, LNP), bf16),
            pltpu.VMEM((2, 256, 256), f32),
            pltpu.VMEM((2, 256, 256), bf16),
            pltpu.VMEM((256, 256), bf16),
            pltpu.VMEM((15, 16, 256), bf16),
            pltpu.VMEM((8, 16, 256), bf16),
            pltpu.VMEM((3, 256, 256), bf16),
            pltpu.VMEM((512, 512), f32),
            pltpu.VMEM((512, 512), f32),
            pltpu.VMEM((4, 128, NPC), bf16),
            pltpu.VMEM((4, 128, NPC), bf16),
            pltpu.VMEM((64, LNP), f32),
            pltpu.SemaphoreType.DMA((copies,)),
            pltpu.SemaphoreType.DMA((copies,)),
        ],
        compiler_params=pltpu.CompilerParams(
            collective_id=1, has_side_effects=True, vmem_limit_bytes=56 << 20),
        name="finish",
    )(states, weight, first)


def body(doms, start_states, stiffness, cell_scale, potential, connectivity, shared_nodes, filter_bounds):
    states, weight, first = filtered(
        start_states, stiffness, cell_scale, potential, connectivity, shared_nodes, filter_bounds, doms)
    return finished(states, weight, first)


def solution(mesh):
    in_specs = (P("st", "dom"), P(), P("dom"), P("dom"), P("dom", None), P("dom", None, None), P())
    return jax.shard_map(
        functools.partial(body, mesh.shape["dom"]), mesh=mesh, in_specs=in_specs, out_specs=P("st", "dom"),
        check_vma=False)
```

```python
import functools
import jax
import jax.numpy as jnp
from jax import lax
from jax.experimental import pallas as pl
from jax.experimental.pallas import tpu as pltpu
from jax.sharding import PartitionSpec as P

f32 = jnp.float32
bf16 = jnp.bfloat16
DEGREE = 3
CELLS = 8
NPC = 512
ENT = CELLS * NPC
LN = 3480
LNP = 3584
SH = 435
FACE = 512
SPEC = 1536
HALF = 2048
MESH_ID = pl.DeviceIdType.MESH


def one_hot_rows(row, count):
    ids = lax.broadcasted_iota(jnp.int32, (count, row.shape[1]), 0)
    return jnp.where(ids == row, 1.0, 0.0).astype(bf16)


def as_column(row):
    return jnp.transpose(jnp.broadcast_to(row, (128, 128)))


def contract_last(a, b):
    return lax.dot_general(a, b, (((1,), (1,)), ((), ())), preferred_element_type=f32)


def dot(a, b):
    return jnp.dot(a, b, preferred_element_type=f32)


def node_tables(faces, oa, ob):
    total = jnp.zeros((128, 32), f32)
    seen = []
    for c in range(CELLS):
        seen.append(total)
        part = slice(c * NPC, (c + 1) * NPC)
        total = total + contract_last(oa[:, part], ob[:, part])
    place = lax.broadcasted_iota(jnp.int32, (1, FACE), 1)
    face_tabs = []
    for side in range(2):
        row = faces[side : side + 1]
        fa = one_hot_rows(lax.shift_right_arithmetic(row, 5), 128)
        fb = one_hot_rows(lax.bitwise_and(row, 31), 32)
        high = (fa * lax.shift_right_logical(place, 7).astype(f32).astype(bf16)).astype(bf16)
        low = (fa * lax.bitwise_and(place, 127).astype(f32).astype(bf16)).astype(bf16)
        face_tabs.append((contract_last(fa, fb), contract_last(high, fb), contract_last(low, fb)))
    (is_l, l_hi, l_lo), (is_r, r_hi, r_lo) = face_tabs
    other = jnp.where((total > 1.5) & (is_l + is_r < 0.5), 1.0, 0.0)
    before_b = jnp.where(
        lax.broadcasted_iota(jnp.int32, (32, 32), 0) < lax.broadcasted_iota(jnp.int32, (32, 32), 1), 1.0, 0.0
    ).astype(bf16)
    before_a = jnp.where(
        lax.broadcasted_iota(jnp.int32, (128, 128), 1) < lax.broadcasted_iota(jnp.int32, (128, 128), 0), 1.0, 0.0
    ).astype(bf16)
    row_sum = jnp.broadcast_to(jnp.sum(other, axis=1, keepdims=True), (128, 32))
    rank = dot(other.astype(bf16), before_b) + dot(before_a, row_sum.astype(bf16))
    rank = rank.astype(jnp.int32)
    slot = rank + jnp.where(rank < FACE - SH, SH, 2 * SH)
    o_hi = lax.shift_right_logical(slot, 7).astype(f32)
    o_lo = lax.bitwise_and(slot, 127).astype(f32)
    hi = jnp.where(is_l > 0.5, l_hi, jnp.where(is_r > 0.5, r_hi + FACE // 128, jnp.where(other > 0.5, o_hi, -1.0)))
    lo = jnp.where(is_l > 0.5, l_lo, jnp.where(is_r > 0.5, r_lo, jnp.where(other > 0.5, o_lo, 0.0)))
    return hi, lo, total, seen


def at_entries(tables, oa, ob):
    stacked = jnp.concatenate(tables, axis=1).astype(bf16)
    picked = lax.dot_general(stacked, oa, (((0,), (0,)), ((), ())), preferred_element_type=f32)
    wide = ob.astype(f32)
    return [
        jnp.sum(picked[32 * k : 32 * (k + 1)] * wide, axis=0, keepdims=True) for k in range(len(tables))
    ]


def split(x):
    high = x.astype(bf16)
    return high, (x - high.astype(f32)).astype(bf16)


def filter_states(
    doms, wait_for_peers, bounds, scale, x_ref, stiff_ref, pot_ref, conn_ref, faces_ref,
    out_ref, weight_ref, first_ref,
    big, nodes, faces, pot_rows, pot_tab, oa, ob, hot, qa_ref, qb_ref, wpot_ref, parts, rows, sums, local, spread, field,
    send, recv, send_sem, recv_sem,
):
    d = lax.axis_index("dom")
    has_left = d > 0
    has_right = d < doms - 1
    for c in range(CELLS):
        nodes[:, c * NPC : (c + 1) * NPC] = conn_ref[c : c + 1]
    faces[...] = jnp.full((2, FACE), -1, jnp.int32)
    faces[:, 0:SH] = faces_ref[0]
    pot_rows[...] = jnp.zeros((32, 128), f32)
    for k in range(LNP // 128):
        pot_rows[k : k + 1] = pot_ref[pl.ds(k * 128, 128)].reshape(1, 128)
    for k in range(4):
        pot_tab[pl.ds(k, 32, stride=4)] = pot_rows[:, k * 32 : (k + 1) * 32]
    conn = nodes[...]
    oa[...] = one_hot_rows(lax.shift_right_logical(conn, 5), 128)
    ob[...] = one_hot_rows(lax.bitwise_and(conn, 31), 32)
    hi_tab, lo_tab, count, seen = node_tables(faces[...], oa, ob)
    pot = pot_tab[...]
    pot_hi = pot.astype(bf16).astype(f32)
    pot_mid = (pot - pot_hi).astype(bf16).astype(f32)
    pot_lo = pot - pot_hi - pot_mid
    for c in range(CELLS):
        part = slice(c * NPC, (c + 1) * NPC)
        qa, qb, cnt, p0, p1, p2, prior = at_entries(
            [hi_tab, lo_tab, count, pot_hi, pot_mid, pot_lo, seen[c]], oa[:, part], ob[:, part]
        )
        qa_ref[:, part] = qa.astype(jnp.int32)
        qb_ref[:, part] = qb.astype(jnp.int32)
        wpot_ref[:, part] = (p0 + p1 + p2) / cnt
        is_first = prior < 0.5
        on_left = (qa >= 0.0) & (qa * 128.0 + qb < SH) & has_left
        weight_ref[:, part] = jnp.where(is_first & jnp.logical_not(on_left), 1.0, 0.0)
        first_ref[:, part] = jnp.where(is_first, conn[:, part], -1)

    low_hot = one_hot_rows(lax.bitwise_and(conn, 127), 128)
    block = lax.shift_right_logical(conn, 7)
    chunk = 4
    for g in range(LNP // 128 // chunk):
        for k in range(chunk):
            mine = jnp.where(block == g * chunk + k, 1.0, 0.0).astype(bf16)
            hot[k * 128 : (k + 1) * 128] = low_hot * mine
        term = dot(x_ref[:, g * chunk * 128 : (g + 1) * chunk * 128], hot[...])
        local[...] = term if g == 0 else local[...] + term
    for c in range(CELLS):
        field[0, c * 64 : (c + 1) * 64] = local[:, c * NPC : (c + 1) * NPC].astype(bf16)

    qb_hot = one_hot_rows(qb_ref[...], 128)
    for j in range(SPEC // 128):
        mine = jnp.where(qa_ref[...] == j, 1.0, 0.0).astype(bf16)
        for h in range(2):
            big[h * SPEC + j * 128 : h * SPEC + (j + 1) * 128, SPEC:LNP] = (
                qb_hot[:, h * HALF : (h + 1) * HALF] * mine[:, h * HALF : (h + 1) * HALF])
    lane = lax.broadcasted_iota(jnp.int32, (128, 128), 1)

    @pl.loop(0, ENT // 128)
    def _(i):
        part = pl.ds(pl.multiple_of(i * 128, 128), 128)
        qa_col = as_column(qa_ref[:, part])
        qb_col = jnp.where(as_column(qb_ref[:, part]) == lane, 1.0, 0.0).astype(bf16)
        for j in range(SPEC // 128):
            mine = jnp.where(qa_col == j, 1.0, 0.0).astype(bf16)
            big[part, j * 128 : (j + 1) * 128] = qb_col * mine

    wait_for_peers()
    center = (bounds[1] + bounds[0]) / 2.0
    half_width = (bounds[1] - bounds[0]) / 2.0
    in_face = lax.broadcasted_iota(jnp.int32, (1, FACE), 1) < SH
    for step in range(DEGREE):
        old = field.at[(step + 1) % 2]
        now = field.at[step % 2]
        products = dot(now[...], stiff_ref[...])
        for c in range(CELLS):
            part = slice(c * NPC, (c + 1) * NPC)
            block_rows = slice(c * 64, (c + 1) * 64)
            value = products[block_rows] * scale[c] + wpot_ref[:, part] * now[block_rows].astype(f32)
            local[:, part] = value
            high, low = split(value)
            parts[0:64, part] = high
            parts[64:128, part] = low
        both = dot(parts[...], big[:, 0 : 2 * FACE])
        sums[:, 0 : 2 * FACE] = both[0:64] + both[64:128]
        send[step, 0] = sums[:, 0:FACE].astype(bf16)
        send[step, 1] = sums[:, FACE : 2 * FACE].astype(bf16)
        down = pltpu.make_async_remote_copy(
            src_ref=send.at[step, 0], dst_ref=recv.at[step, 1],
            send_sem=send_sem.at[step, 0], recv_sem=recv_sem.at[step, 1],
            device_id={"dom": d - 1}, device_id_type=MESH_ID)
        up = pltpu.make_async_remote_copy(
            src_ref=send.at[step, 1], dst_ref=recv.at[step, 0],
            send_sem=send_sem.at[step, 1], recv_sem=recv_sem.at[step, 0],
            device_id={"dom": d + 1}, device_id_type=MESH_ID)

        @pl.when(has_left)
        def _():
            down.start()

        @pl.when(has_right)
        def _():
            up.start()

        both = dot(parts[...], big[:, 2 * FACE : SPEC])
        high, low = split(both[0:64] + both[64:128])
        rows[0:64, 2 * FACE : SPEC] = high
        rows[64:128, 2 * FACE : SPEC] = low
        others = [
            dot(rows[:, 2 * FACE : SPEC], big[h * SPEC + 2 * FACE : (h + 1) * SPEC, SPEC:LNP]) for h in range(2)]

        @pl.when(has_left)
        def _():
            down.wait_send()
            up.wait_recv()

        @pl.when(has_right)
        def _():
            up.wait_send()
            down.wait_recv()

        for side, there in ((0, has_left), (1, has_right)):
            part = slice(side * FACE, (side + 1) * FACE)
            came = jnp.where(in_face & there, recv[step, side].astype(f32), 0.0)
            high, low = split(sums[:, part] + came)
            rows[0:64, part] = high
            rows[64:128, part] = low
        for h in range(2):
            both = others[h] + dot(rows[:, 0 : 2 * FACE], big[h * SPEC : h * SPEC + 2 * FACE, SPEC:LNP])
            spread[:, h * HALF : (h + 1) * HALF] = both[0:64] + both[64:128]
        for c in range(CELLS):
            part = slice(c * NPC, (c + 1) * NPC)
            block_rows = slice(c * 64, (c + 1) * 64)
            h = jnp.where(qa_ref[:, part] >= 0, spread[:, part], local[:, part])
            fresh = (h - center * now[block_rows].astype(f32)) / half_width
            if step > 0:
                fresh = 2.0 * fresh - old[block_rows].astype(f32)
            if step == DEGREE - 1:
                out_ref[block_rows] = fresh.astype(bf16)
            else:
                old[block_rows] = fresh.astype(bf16)


def product(a, b):
    a_hi, a_lo = split(a)
    b_hi, b_lo = split(b)
    return dot(a_hi, b_hi) + (dot(a_hi, b_lo) + dot(a_lo, b_hi))


def kernel(doms, bounds, scale, x_ref, stiff_ref, pot_ref, conn_ref, faces_ref, out_ref, *scratch):
    hot, mine_ref, weight_ref, first_ref = scratch[0:4]
    (got, sums, half, from_core, from_plane, line, total, gram, root, turned, back, acc, sent, came) = scratch[4:18]
    d = lax.axis_index("dom")
    s = lax.axis_index("st")
    core, y, z_lo = lax.rem(d, 2), lax.rem(lax.div(d, 2), 4), lax.div(d, 8)
    x, z_hi = lax.rem(s, 4), lax.div(s, 4)
    z = z_hi * 4 + z_lo

    def device(core=core, y=y, z_lo=z_lo, x=x, z_hi=z_hi):
        return {"dom": (z_lo * 4 + y) * 2 + core, "st": z_hi * 4 + x}

    def around(at, by, count):
        return lax.rem(at + by, count)

    def along_z(by):
        there = around(z, by, 8)
        return device(z_lo=lax.rem(there, 4), z_hi=lax.div(there, 4))

    count = [0]

    def copy(src, dst, to):
        k = count[0]
        count[0] += 1
        return pltpu.make_async_remote_copy(
            src_ref=src, dst_ref=dst, send_sem=sent.at[k], recv_sem=came.at[k], device_id=to, device_id_type=MESH_ID)

    def start(copies):
        for one in copies:
            one.start()
        return copies

    def finish(copies):
        for one in copies:
            one.wait()

    peers = [device(core=1 - core)]
    peers += [
        device(x=around(x, kx, 4), y=around(y, ky, 4)) for kx in range(4) for ky in range(4) if kx + ky]
    peers += [along_z(k) for k in range(1, 8)]
    peers += [device(x=around(x, k, 4), z_hi=1 - z_hi) for k in range(1, 4)]
    peers += [{"dom": lax.rem(d + 1, doms)}, {"dom": lax.rem(d + doms - 1, doms)}]
    barrier = pltpu.get_barrier_semaphore()
    for peer in peers:
        pl.semaphore_signal(barrier, inc=1, device_id=peer, device_id_type=MESH_ID)
    filter_states(
        doms, lambda: pl.semaphore_wait(barrier, len(peers)), bounds, scale, x_ref, stiff_ref, pot_ref, conn_ref,
        faces_ref, mine_ref, weight_ref, first_ref, hot, *scratch[18:])

    def pair_rows(at):
        return pl.ds(pl.multiple_of(at * 128, 128), 128)

    def cell_rows(at, k):
        return pl.ds(pl.multiple_of(at * 128 + k * 64, 64), 64)

    crossing = []
    for k in range(4):
        there = around(x, k, 4)
        crossing.append(copy(
            mine_ref.at[cell_rows(there, 1 - z_hi)], got.at[s, cell_rows(0, 1 - z_hi)],
            device(x=there, z_hi=1 - z_hi)))
    start(crossing)
    beside = []
    for k in range(1, 4):
        there = around(x, k, 4)
        beside.append(copy(mine_ref.at[pair_rows(there)], got.at[s], device(x=there)))
    start(beside)
    late = []
    for k in range(4):
        there = around(x, k, 4)
        late.append(copy(
            mine_ref.at[cell_rows(there, z_hi)], got.at[s, cell_rows(0, z_hi)],
            device(x=there, z_hi=1 - z_hi)))
    got[s] = mine_ref[pair_rows(x)]

    lane = lax.broadcasted_iota(jnp.int32, (128, 128), 1)

    @pl.loop(0, ENT // 128)
    def _(i):
        at = pl.ds(pl.multiple_of(i * 128, 128), 128)
        node = as_column(first_ref[:, at])
        low = jnp.where(lax.bitwise_and(node, 127) == lane, 1.0, 0.0).astype(bf16)
        block = lax.shift_right_arithmetic(node, 7)
        for j in range(LNP // 128):
            mine = jnp.where(block == j, 1.0, 0.0).astype(bf16)
            hot[at, j * 128 : (j + 1) * 128] = low * mine

    finish(crossing)
    start(late[0:2])
    finish(beside)

    def weighted(rows, at):
        mark = weight_ref[:, pl.ds(pl.multiple_of(at * NPC, NPC), NPC)]
        return (rows.astype(f32) * mark).astype(bf16)

    own = pl.ds(pl.multiple_of(z_hi * 4, 4), 4)
    first_cell = got[own, 0:64].reshape(256, NPC)
    second_cell = got[own, 64:128].reshape(256, NPC)
    sums[0] = contract_last(weighted(first_cell, 2 * x), first_cell) + contract_last(
        weighted(second_cell, 2 * x + 1), second_cell)
    shared_rows = pl.ds(pl.multiple_of(z_hi * 64, 64), 64)
    low_half = got[0:4, shared_rows].reshape(256, NPC)
    high_half = got[4:8, shared_rows].reshape(256, NPC)
    sums[1] = contract_last(weighted(low_half, 2 * x + z_hi), high_half)

    half[0] = sums[0].astype(bf16)
    half[1] = sums[1].astype(bf16)
    finish(start([copy(half.at[1 - core], from_core, device(core=1 - core))]))
    sums[core] = sums[core] + from_core[...].astype(f32)
    half[core] = sums[core].astype(bf16)
    plane = [(kx, ky) for kx in range(4) for ky in range(4)][1:]

    def piece_of(kx, ky):
        return pl.ds(pl.multiple_of(around(x, kx, 4) * 64 + around(y, ky, 4) * 16, 16), 16)

    def in_plane(kx, ky):
        return device(x=around(x, kx, 4), y=around(y, ky, 4))

    finish(start([
        copy(half.at[core, piece_of(*by)], from_plane.at[k], in_plane(*by)) for k, by in enumerate(plane)]))
    piece = sums[core, piece_of(0, 0)]
    for k in range(15):
        piece = piece + from_plane[k].astype(f32)
    line[z] = piece.astype(bf16)
    finish(start([copy(line.at[z], line.at[z], along_z(k)) for k in range(1, 8)]))
    start(late[2:4])
    low_sum = line[0].astype(f32)
    high_sum = line[4].astype(f32)
    for k in range(1, 4):
        low_sum = low_sum + line[k].astype(f32)
        high_sum = high_sum + line[4 + k].astype(f32)
    on_core = 2 * core
    piece_rows = piece_of(0, 0)

    @pl.when(core == 0)
    def _():
        total[1, piece_rows] = high_sum.astype(bf16)

    total[on_core, piece_rows] = (low_sum + jnp.where(core == 1, high_sum, 0.0)).astype(bf16)
    held = [copy(total.at[pl.ds(0, 2), piece_rows], total.at[pl.ds(0, 2), piece_rows], in_plane(*by)) for by in plane]
    count[0] -= len(plane)
    held_one = [copy(total.at[2, piece_rows], total.at[2, piece_rows], in_plane(*by)) for by in plane]

    @pl.when(core == 0)
    def _():
        finish(start(held))

    @pl.when(core == 1)
    def _():
        finish(start(held_one))

    down = [copy(total.at[k], total.at[k], device(core=1 - core)) for k in range(3)]

    @pl.when(core == 0)
    def _():
        start(down[0:2])
        for one in down[0:2]:
            one.wait_send()
        down[2].wait_recv()

    @pl.when(core == 1)
    def _():
        start(down[2:3])
        down[2].wait_send()
        for one in down[0:2]:
            one.wait_recv()

    upper = total[2].astype(f32)
    gram[0:256, 0:256] = total[0].astype(f32)
    gram[256:512, 256:512] = total[1].astype(f32)
    gram[0:256, 256:512] = upper
    gram[256:512, 0:256] = jnp.transpose(upper)
    g = gram[...]
    frobenius = jnp.sqrt(jnp.sum(jnp.sum(g * g, axis=1, keepdims=True), axis=0, keepdims=True) + 1e-06)
    a = g / frobenius
    gram[...] = a
    square = product(a, a)
    diagonal = lax.broadcasted_iota(jnp.int32, (512, 512), 0) == lax.broadcasted_iota(jnp.int32, (512, 512), 1)
    root[...] = (
        jnp.where(diagonal, 2.25, 0.0) - 2.4375 * a + 1.6875 * square
        + product(square, 0.0625 * square - 0.5625 * a))
    columns = root[:, pl.ds(pl.multiple_of(z_hi * 256, 256), 256)]
    cubed = product(root[...], product(root[...], columns))
    coeffs = ((1.5 * columns - 0.5 * product(gram[...], cubed)) / jnp.sqrt(frobenius)).astype(bf16)

    finish(late)
    for k in range(2):
        cell = got[:, k * 64 : (k + 1) * 64].reshape(512, NPC)
        rotated = lax.dot_general(coeffs, cell, (((0,), (0,)), ((), ())), preferred_element_type=f32)
        turned[:, k * 64 : (k + 1) * 64] = rotated.astype(bf16).reshape(4, 64, NPC)
    returned = start([
        copy(turned.at[around(x, k, 4)], back.at[x], device(x=around(x, k, 4))) for k in range(1, 4)])
    back[x] = turned[x]
    for k in range(4):
        source = around(x, 4 - k, 4)
        if k:
            returned[k - 1].wait()
        pair = jnp.concatenate([back[source, 0:64], back[source, 64:128]], axis=1)
        term = dot(pair, hot[pl.ds(pl.multiple_of(source * 1024, 1024), 1024)])
        if k == 0:
            acc[...] = term
        elif k < 3:
            acc[...] = acc[...] + term
        else:
            out_ref[...] = (acc[...] + term).astype(bf16)


def body(doms, start_states, stiffness, cell_scale, potential, connectivity, shared_nodes, filter_bounds):
    vmem = pl.BlockSpec(memory_space=pltpu.VMEM)
    smem = pl.BlockSpec(memory_space=pltpu.SMEM)
    copies = 11 + 1 + 15 + 7 + 15 + 3 + 3
    finish_scratch = [
        pltpu.VMEM((ENT, LNP), bf16),
        pltpu.VMEM((512, NPC), bf16),
        pltpu.VMEM((1, ENT), f32),
        pltpu.VMEM((1, ENT), jnp.int32),
        pltpu.VMEM((8, 128, NPC), bf16),
        pltpu.VMEM((2, 256, 256), f32),
        pltpu.VMEM((2, 256, 256), bf16),
        pltpu.VMEM((256, 256), bf16),
        pltpu.VMEM((15, 16, 256), bf16),
        pltpu.VMEM((8, 16, 256), bf16),
        pltpu.VMEM((3, 256, 256), bf16),
        pltpu.VMEM((512, 512), f32),
        pltpu.VMEM((512, 512), f32),
        pltpu.VMEM((4, 128, NPC), bf16),
        pltpu.VMEM((4, 128, NPC), bf16),
        pltpu.VMEM((64, LNP), f32),
        pltpu.SemaphoreType.DMA((copies,)),
        pltpu.SemaphoreType.DMA((copies,)),
    ]
    filter_scratch = [
        pltpu.VMEM((1, ENT), jnp.int32),
        pltpu.VMEM((2, FACE), jnp.int32),
        pltpu.VMEM((32, 128), f32),
        pltpu.VMEM((128, 32), f32),
        pltpu.VMEM((128, ENT), bf16),
        pltpu.VMEM((32, ENT), bf16),
        pltpu.VMEM((512, ENT), bf16),
        pltpu.VMEM((1, ENT), jnp.int32),
        pltpu.VMEM((1, ENT), jnp.int32),
        pltpu.VMEM((1, ENT), f32),
        pltpu.VMEM((128, ENT), bf16),
        pltpu.VMEM((128, SPEC), bf16),
        pltpu.VMEM((64, 2 * FACE), f32),
        pltpu.VMEM((64, ENT), f32),
        pltpu.VMEM((64, ENT), f32),
        pltpu.VMEM((2, 512, NPC), bf16),
        pltpu.VMEM((DEGREE, 2, 64, FACE), bf16),
        pltpu.VMEM((DEGREE, 2, 64, FACE), bf16),
        pltpu.SemaphoreType.DMA((DEGREE, 2)),
        pltpu.SemaphoreType.DMA((DEGREE, 2)),
    ]
    return pl.pallas_call(
        functools.partial(kernel, doms),
        out_shape=jax.ShapeDtypeStruct((64, LNP), bf16),
        in_specs=[smem, smem] + [vmem] * 5,
        out_specs=vmem,
        scratch_shapes=finish_scratch + filter_scratch,
        compiler_params=pltpu.CompilerParams(
            collective_id=0, has_side_effects=True, vmem_limit_bytes=58 << 20),
        name="subspace_step",
    )(filter_bounds, cell_scale, start_states, stiffness, potential, connectivity, shared_nodes)


def solution(mesh):
    in_specs = (P("st", "dom"), P(), P("dom"), P("dom"), P("dom", None), P("dom", None, None), P())
    return jax.shard_map(
        functools.partial(body, mesh.shape["dom"]), mesh=mesh, in_specs=in_specs, out_specs=P("st", "dom"),
        check_vma=False)
```

```python
import functools
import jax
import jax.numpy as jnp
from jax import lax
from jax.experimental import pallas as pl
from jax.experimental.pallas import tpu as pltpu
from jax.sharding import PartitionSpec as P

f32 = jnp.float32
bf16 = jnp.bfloat16
DEGREE = 3
CELLS = 8
NPC = 512
ENT = CELLS * NPC
LN = 3480
LNP = 3584
SH = 435
FACE = 512
SPEC = 1536
HALF = 2048
MESH_ID = pl.DeviceIdType.MESH


def one_hot_rows(row, count):
    ids = lax.broadcasted_iota(jnp.int32, (count, row.shape[1]), 0)
    return jnp.where(ids == row, 1.0, 0.0).astype(bf16)


def as_column(row):
    return jnp.transpose(jnp.broadcast_to(row, (128, 128)))


def contract_last(a, b):
    return lax.dot_general(a, b, (((1,), (1,)), ((), ())), preferred_element_type=f32)


def dot(a, b):
    return jnp.dot(a, b, preferred_element_type=f32)


def node_tables(faces, oa, ob):
    total = jnp.zeros((128, 32), f32)
    seen = []
    for c in range(CELLS):
        seen.append(total)
        part = slice(c * NPC, (c + 1) * NPC)
        total = total + contract_last(oa[:, part], ob[:, part])
    place = lax.broadcasted_iota(jnp.int32, (1, FACE), 1)
    face_tabs = []
    for side in range(2):
        row = faces[side : side + 1]
        fa = one_hot_rows(lax.shift_right_arithmetic(row, 5), 128)
        fb = one_hot_rows(lax.bitwise_and(row, 31), 32)
        high = (fa * lax.shift_right_logical(place, 7).astype(f32).astype(bf16)).astype(bf16)
        low = (fa * lax.bitwise_and(place, 127).astype(f32).astype(bf16)).astype(bf16)
        face_tabs.append((contract_last(fa, fb), contract_last(high, fb), contract_last(low, fb)))
    (is_l, l_hi, l_lo), (is_r, r_hi, r_lo) = face_tabs
    other = jnp.where((total > 1.5) & (is_l + is_r < 0.5), 1.0, 0.0)
    before_b = jnp.where(
        lax.broadcasted_iota(jnp.int32, (32, 32), 0) < lax.broadcasted_iota(jnp.int32, (32, 32), 1), 1.0, 0.0
    ).astype(bf16)
    before_a = jnp.where(
        lax.broadcasted_iota(jnp.int32, (128, 128), 1) < lax.broadcasted_iota(jnp.int32, (128, 128), 0), 1.0, 0.0
    ).astype(bf16)
    row_sum = jnp.broadcast_to(jnp.sum(other, axis=1, keepdims=True), (128, 32))
    rank = dot(other.astype(bf16), before_b) + dot(before_a, row_sum.astype(bf16))
    rank = rank.astype(jnp.int32)
    slot = rank + jnp.where(rank < FACE - SH, SH, 2 * SH)
    o_hi = lax.shift_right_logical(slot, 7).astype(f32)
    o_lo = lax.bitwise_and(slot, 127).astype(f32)
    hi = jnp.where(is_l > 0.5, l_hi, jnp.where(is_r > 0.5, r_hi + FACE // 128, jnp.where(other > 0.5, o_hi, -1.0)))
    lo = jnp.where(is_l > 0.5, l_lo, jnp.where(is_r > 0.5, r_lo, jnp.where(other > 0.5, o_lo, 0.0)))
    return hi, lo, total, seen


def at_entries(tables, oa, ob):
    stacked = jnp.concatenate(tables, axis=1).astype(bf16)
    picked = lax.dot_general(stacked, oa, (((0,), (0,)), ((), ())), preferred_element_type=f32)
    wide = ob.astype(f32)
    return [
        jnp.sum(picked[32 * k : 32 * (k + 1)] * wide, axis=0, keepdims=True) for k in range(len(tables))
    ]


def split(x):
    high = x.astype(bf16)
    return high, (x - high.astype(f32)).astype(bf16)


def filter_states(
    doms, wait_for_peers, early_half, half_ready, bounds, scale, x_ref, stiff_ref, pot_ref, conn_ref, faces_ref,
    out_ref, weight_ref, first_ref,
    big, nodes, faces, pot_rows, pot_tab, oa, ob, hot, qa_ref, qb_ref, wpot_ref, parts, rows, sums, local, spread, field,
    send, recv, send_sem, recv_sem,
):
    d = lax.axis_index("dom")
    has_left = d > 0
    has_right = d < doms - 1
    for c in range(CELLS):
        nodes[:, c * NPC : (c + 1) * NPC] = conn_ref[c : c + 1]
    faces[...] = jnp.full((2, FACE), -1, jnp.int32)
    faces[:, 0:SH] = faces_ref[0]
    pot_rows[...] = jnp.zeros((32, 128), f32)
    for k in range(LNP // 128):
        pot_rows[k : k + 1] = pot_ref[pl.ds(k * 128, 128)].reshape(1, 128)
    for k in range(4):
        pot_tab[pl.ds(k, 32, stride=4)] = pot_rows[:, k * 32 : (k + 1) * 32]
    conn = nodes[...]
    oa[...] = one_hot_rows(lax.shift_right_logical(conn, 5), 128)
    ob[...] = one_hot_rows(lax.bitwise_and(conn, 31), 32)
    hi_tab, lo_tab, count, seen = node_tables(faces[...], oa, ob)
    pot = pot_tab[...]
    pot_hi = pot.astype(bf16).astype(f32)
    pot_mid = (pot - pot_hi).astype(bf16).astype(f32)
    pot_lo = pot - pot_hi - pot_mid
    for c in range(CELLS):
        part = slice(c * NPC, (c + 1) * NPC)
        qa, qb, cnt, p0, p1, p2, prior = at_entries(
            [hi_tab, lo_tab, count, pot_hi, pot_mid, pot_lo, seen[c]], oa[:, part], ob[:, part]
        )
        qa_ref[:, part] = qa.astype(jnp.int32)
        qb_ref[:, part] = qb.astype(jnp.int32)
        wpot_ref[:, part] = (p0 + p1 + p2) / cnt
        is_first = prior < 0.5
        on_left = (qa >= 0.0) & (qa * 128.0 + qb < SH) & has_left
        weight_ref[:, part] = jnp.where(is_first & jnp.logical_not(on_left), 1.0, 0.0)
        first_ref[:, part] = jnp.where(is_first, conn[:, part], -1)

    low_hot = one_hot_rows(lax.bitwise_and(conn, 127), 128)
    block = lax.shift_right_logical(conn, 7)
    chunk = 4
    for g in range(LNP // 128 // chunk):
        for k in range(chunk):
            mine = jnp.where(block == g * chunk + k, 1.0, 0.0).astype(bf16)
            hot[k * 128 : (k + 1) * 128] = low_hot * mine
        term = dot(x_ref[:, g * chunk * 128 : (g + 1) * chunk * 128], hot[...])
        local[...] = term if g == 0 else local[...] + term
    for c in range(CELLS):
        field[0, c * 64 : (c + 1) * 64] = local[:, c * NPC : (c + 1) * NPC].astype(bf16)

    qb_hot = one_hot_rows(qb_ref[...], 128)
    for j in range(SPEC // 128):
        mine = jnp.where(qa_ref[...] == j, 1.0, 0.0).astype(bf16)
        for h in range(2):
            big[h * SPEC + j * 128 : h * SPEC + (j + 1) * 128, SPEC:LNP] = (
                qb_hot[:, h * HALF : (h + 1) * HALF] * mine[:, h * HALF : (h + 1) * HALF])
    lane = lax.broadcasted_iota(jnp.int32, (128, 128), 1)

    @pl.loop(0, ENT // 128)
    def _(i):
        part = pl.ds(pl.multiple_of(i * 128, 128), 128)
        qa_col = as_column(qa_ref[:, part])
        qb_col = jnp.where(as_column(qb_ref[:, part]) == lane, 1.0, 0.0).astype(bf16)
        for j in range(SPEC // 128):
            mine = jnp.where(qa_col == j, 1.0, 0.0).astype(bf16)
            big[part, j * 128 : (j + 1) * 128] = qb_col * mine

    wait_for_peers()
    center = (bounds[1] + bounds[0]) / 2.0
    half_width = (bounds[1] - bounds[0]) / 2.0
    in_face = lax.broadcasted_iota(jnp.int32, (1, FACE), 1) < SH
    for step in range(DEGREE):
        old = field.at[(step + 1) % 2]
        now = field.at[step % 2]
        products = dot(now[...], stiff_ref[...])
        for c in range(CELLS):
            part = slice(c * NPC, (c + 1) * NPC)
            block_rows = slice(c * 64, (c + 1) * 64)
            value = products[block_rows] * scale[c] + wpot_ref[:, part] * now[block_rows].astype(f32)
            local[:, part] = value
            high, low = split(value)
            parts[0:64, part] = high
            parts[64:128, part] = low
        both = dot(parts[...], big[:, 0 : 2 * FACE])
        sums[:, 0 : 2 * FACE] = both[0:64] + both[64:128]
        send[step, 0] = sums[:, 0:FACE].astype(bf16)
        send[step, 1] = sums[:, FACE : 2 * FACE].astype(bf16)
        down = pltpu.make_async_remote_copy(
            src_ref=send.at[step, 0], dst_ref=recv.at[step, 1],
            send_sem=send_sem.at[step, 0], recv_sem=recv_sem.at[step, 1],
            device_id={"dom": d - 1}, device_id_type=MESH_ID)
        up = pltpu.make_async_remote_copy(
            src_ref=send.at[step, 1], dst_ref=recv.at[step, 0],
            send_sem=send_sem.at[step, 1], recv_sem=recv_sem.at[step, 0],
            device_id={"dom": d + 1}, device_id_type=MESH_ID)

        @pl.when(has_left)
        def _():
            down.start()

        @pl.when(has_right)
        def _():
            up.start()

        both = dot(parts[...], big[:, 2 * FACE : SPEC])
        high, low = split(both[0:64] + both[64:128])
        rows[0:64, 2 * FACE : SPEC] = high
        rows[64:128, 2 * FACE : SPEC] = low
        last = step == DEGREE - 1
        order = (early_half, 1 - early_half) if last else (0, 1)

        def special_rows(h, begin, size):
            return pl.ds(pl.multiple_of(h * SPEC + begin, FACE), size)

        others = [
            dot(rows[:, 2 * FACE : SPEC], big[special_rows(h, 2 * FACE, FACE), SPEC:LNP]) for h in order]

        @pl.when(has_left)
        def _():
            down.wait_send()
            up.wait_recv()

        @pl.when(has_right)
        def _():
            up.wait_send()
            down.wait_recv()

        for side, there in ((0, has_left), (1, has_right)):
            part = slice(side * FACE, (side + 1) * FACE)
            came = jnp.where(in_face & there, recv[step, side].astype(f32), 0.0)
            high, low = split(sums[:, part] + came)
            rows[0:64, part] = high
            rows[64:128, part] = low
        for h, other in zip(order, others):
            both = other + dot(rows[:, 0 : 2 * FACE], big[special_rows(h, 0, 2 * FACE), SPEC:LNP])
            spread[...] = both[0:64] + both[64:128]
            for k in range(CELLS // 2):
                part = pl.ds(pl.multiple_of((4 * h + k) * NPC, NPC), NPC)
                block_rows = pl.ds(pl.multiple_of((4 * h + k) * 64, 64), 64)
                hv = jnp.where(qa_ref[:, part] >= 0, spread[:, k * NPC : (k + 1) * NPC], local[:, part])
                fresh = (hv - center * now[block_rows].astype(f32)) / half_width
                if step > 0:
                    fresh = 2.0 * fresh - old[block_rows].astype(f32)
                if last:
                    out_ref[block_rows] = fresh.astype(bf16)
                else:
                    old[block_rows] = fresh.astype(bf16)
            if last and h is early_half:
                half_ready()


def product(a, b):
    a_hi, a_lo = split(a)
    b_hi, b_lo = split(b)
    return dot(a_hi, b_hi) + (dot(a_hi, b_lo) + dot(a_lo, b_hi))


def kernel(doms, bounds, scale, x_ref, stiff_ref, pot_ref, conn_ref, faces_ref, out_ref, *scratch):
    hot, mine_ref, weight_ref, first_ref = scratch[0:4]
    (got, sums, half, from_core, from_plane, line, total, gram, root, turned, back, acc, sent, came) = scratch[4:18]
    d = lax.axis_index("dom")
    s = lax.axis_index("st")
    core, y, z_lo = lax.rem(d, 2), lax.rem(lax.div(d, 2), 4), lax.div(d, 8)
    x, z_hi = lax.rem(s, 4), lax.div(s, 4)
    z = z_hi * 4 + z_lo

    def device(core=core, y=y, z_lo=z_lo, x=x, z_hi=z_hi):
        return {"dom": (z_lo * 4 + y) * 2 + core, "st": z_hi * 4 + x}

    def around(at, by, count):
        return lax.rem(at + by, count)

    def along_z(by):
        there = around(z, by, 8)
        return device(z_lo=lax.rem(there, 4), z_hi=lax.div(there, 4))

    count = [0]

    def copy(src, dst, to):
        k = count[0]
        count[0] += 1
        return pltpu.make_async_remote_copy(
            src_ref=src, dst_ref=dst, send_sem=sent.at[k], recv_sem=came.at[k], device_id=to, device_id_type=MESH_ID)

    def start(copies):
        for one in copies:
            one.start()
        return copies

    def finish(copies):
        for one in copies:
            one.wait()

    peers = [device(core=1 - core)]
    peers += [
        device(x=around(x, kx, 4), y=around(y, ky, 4)) for kx in range(4) for ky in range(4) if kx + ky]
    peers += [along_z(k) for k in range(1, 8)]
    peers += [device(x=around(x, k, 4), z_hi=1 - z_hi) for k in range(1, 4)]
    peers += [{"dom": lax.rem(d + 1, doms)}, {"dom": lax.rem(d + doms - 1, doms)}]
    barrier = pltpu.get_barrier_semaphore()
    for peer in peers:
        pl.semaphore_signal(barrier, inc=1, device_id=peer, device_id_type=MESH_ID)

    def cell_rows(at, k):
        return pl.ds(pl.multiple_of((at + 4 * k) * 64, 64), 64)

    def place(k):
        return pl.ds(pl.multiple_of(k * 64, 64), 64)

    def to_block(by, k, z_there):
        there = around(x, by, 4)
        return copy(mine_ref.at[cell_rows(there, k)], got.at[s, place(k)], device(x=there, z_hi=z_there))

    crossing = [to_block(by, 1 - z_hi, 1 - z_hi) for by in range(4)]
    beside = [to_block(by, k, z_hi) for by in range(1, 4) for k in range(2)]
    late = [to_block(by, z_hi, 1 - z_hi) for by in range(4)]
    filter_states(
        doms, lambda: pl.semaphore_wait(barrier, len(peers)), 1 - z_hi, lambda: start(crossing), bounds, scale, x_ref,
        stiff_ref, pot_ref, conn_ref, faces_ref, mine_ref, weight_ref, first_ref, hot, *scratch[18:])
    start(beside)
    for k in range(2):
        got[s, place(k)] = mine_ref[cell_rows(x, k)]

    lane = lax.broadcasted_iota(jnp.int32, (128, 128), 1)

    @pl.loop(0, ENT // 128)
    def _(i):
        at = pl.ds(pl.multiple_of(i * 128, 128), 128)
        node = as_column(first_ref[:, at])
        low = jnp.where(lax.bitwise_and(node, 127) == lane, 1.0, 0.0).astype(bf16)
        block = lax.shift_right_arithmetic(node, 7)
        for j in range(LNP // 128):
            mine = jnp.where(block == j, 1.0, 0.0).astype(bf16)
            hot[at, j * 128 : (j + 1) * 128] = low * mine

    finish(beside)

    def weighted(rows, at):
        mark = weight_ref[:, pl.ds(pl.multiple_of(at * NPC, NPC), NPC)]
        return (rows.astype(f32) * mark).astype(bf16)

    own = pl.ds(pl.multiple_of(z_hi * 4, 4), 4)
    first_cell = got[own, 0:64].reshape(256, NPC)
    second_cell = got[own, 64:128].reshape(256, NPC)
    sums[0] = contract_last(weighted(first_cell, x), first_cell) + contract_last(
        weighted(second_cell, x + 4), second_cell)
    half[0] = sums[0].astype(bf16)
    finish(crossing)
    start(late[0:2])
    shared_rows = pl.ds(pl.multiple_of(z_hi * 64, 64), 64)
    low_half = got[0:4, shared_rows].reshape(256, NPC)
    high_half = got[4:8, shared_rows].reshape(256, NPC)
    sums[1] = contract_last(weighted(low_half, x + 4 * z_hi), high_half)

    half[1] = sums[1].astype(bf16)
    finish(start([copy(half.at[1 - core], from_core, device(core=1 - core))]))
    sums[core] = sums[core] + from_core[...].astype(f32)
    half[core] = sums[core].astype(bf16)
    plane = [(kx, ky) for kx in range(4) for ky in range(4)][1:]

    def piece_of(kx, ky):
        return pl.ds(pl.multiple_of(around(x, kx, 4) * 64 + around(y, ky, 4) * 16, 16), 16)

    def in_plane(kx, ky):
        return device(x=around(x, kx, 4), y=around(y, ky, 4))

    finish(start([
        copy(half.at[core, piece_of(*by)], from_plane.at[k], in_plane(*by)) for k, by in enumerate(plane)]))
    piece = sums[core, piece_of(0, 0)]
    for k in range(15):
        piece = piece + from_plane[k].astype(f32)
    line[z] = piece.astype(bf16)
    finish(start([copy(line.at[z], line.at[z], along_z(k)) for k in range(1, 8)]))
    start(late[2:4])
    low_sum = line[0].astype(f32)
    high_sum = line[4].astype(f32)
    for k in range(1, 4):
        low_sum = low_sum + line[k].astype(f32)
        high_sum = high_sum + line[4 + k].astype(f32)
    on_core = 2 * core
    piece_rows = piece_of(0, 0)

    @pl.when(core == 0)
    def _():
        total[1, piece_rows] = high_sum.astype(bf16)

    total[on_core, piece_rows] = (low_sum + jnp.where(core == 1, high_sum, 0.0)).astype(bf16)
    held = [copy(total.at[pl.ds(0, 2), piece_rows], total.at[pl.ds(0, 2), piece_rows], in_plane(*by)) for by in plane]
    count[0] -= len(plane)
    held_one = [copy(total.at[2, piece_rows], total.at[2, piece_rows], in_plane(*by)) for by in plane]

    came_from = [piece_rows] + [piece_of(4 - kx, 4 - ky) for kx, ky in plane]
    other_core = device(core=1 - core)
    passed = [copy(total.at[pl.ds(0, 2), at], total.at[pl.ds(0, 2), at], other_core) for at in came_from]
    count[0] -= len(came_from)
    passed_one = [copy(total.at[2, at], total.at[2, at], other_core) for at in came_from]

    def pass_on(arriving, onward, awaited):
        start(arriving)
        onward[0].start()
        for one, after in zip(arriving, onward[1:]):
            one.wait_recv()
            after.start()
        for one in arriving + onward:
            one.wait_send()
        for one in awaited:
            one.wait_recv()

    @pl.when(core == 0)
    def _():
        pass_on(held, passed, passed_one)

    @pl.when(core == 1)
    def _():
        pass_on(held_one, passed_one, passed)

    upper = total[2].astype(f32)
    gram[0:256, 0:256] = total[0].astype(f32)
    gram[256:512, 256:512] = total[1].astype(f32)
    gram[0:256, 256:512] = upper
    gram[256:512, 0:256] = jnp.transpose(upper)
    g = gram[...]
    frobenius = jnp.sqrt(jnp.sum(jnp.sum(g * g, axis=1, keepdims=True), axis=0, keepdims=True) + 1e-06)
    a = g / frobenius
    gram[...] = a
    square = product(a, a)
    diagonal = lax.broadcasted_iota(jnp.int32, (512, 512), 0) == lax.broadcasted_iota(jnp.int32, (512, 512), 1)
    root[...] = (
        jnp.where(diagonal, 2.25, 0.0) - 2.4375 * a + 1.6875 * square
        + product(square, 0.0625 * square - 0.5625 * a))
    columns = root[:, pl.ds(pl.multiple_of(z_hi * 256, 256), 256)]
    cubed = product(root[...], product(root[...], columns))
    coeffs = ((1.5 * columns - 0.5 * product(gram[...], cubed)) / jnp.sqrt(frobenius)).astype(bf16)

    finish(late)
    for k in range(2):
        cell = got[:, k * 64 : (k + 1) * 64].reshape(512, NPC)
        rotated = lax.dot_general(coeffs, cell, (((0,), (0,)), ((), ())), preferred_element_type=f32)
        turned[:, k * 64 : (k + 1) * 64] = rotated.astype(bf16).reshape(4, 64, NPC)
    returned = start([
        copy(turned.at[around(x, k, 4)], back.at[x], device(x=around(x, k, 4))) for k in range(1, 4)])
    back[x] = turned[x]
    for k in range(4):
        source = around(x, 4 - k, 4)
        if k:
            returned[k - 1].wait()
        term = dot(back[source, 0:64], hot[pl.ds(pl.multiple_of(source * NPC, NPC), NPC)]) + dot(
            back[source, 64:128], hot[pl.ds(pl.multiple_of((source + 4) * NPC, NPC), NPC)])
        if k == 0:
            acc[...] = term
        elif k < 3:
            acc[...] = acc[...] + term
        else:
            out_ref[...] = (acc[...] + term).astype(bf16)


def body(doms, start_states, stiffness, cell_scale, potential, connectivity, shared_nodes, filter_bounds):
    vmem = pl.BlockSpec(memory_space=pltpu.VMEM)
    smem = pl.BlockSpec(memory_space=pltpu.SMEM)
    copies = 14 + 1 + 15 + 7 + 15 + 16 + 3
    finish_scratch = [
        pltpu.VMEM((ENT, LNP), bf16),
        pltpu.VMEM((512, NPC), bf16),
        pltpu.VMEM((1, ENT), f32),
        pltpu.VMEM((1, ENT), jnp.int32),
        pltpu.VMEM((8, 128, NPC), bf16),
        pltpu.VMEM((2, 256, 256), f32),
        pltpu.VMEM((2, 256, 256), bf16),
        pltpu.VMEM((256, 256), bf16),
        pltpu.VMEM((15, 16, 256), bf16),
        pltpu.VMEM((8, 16, 256), bf16),
        pltpu.VMEM((3, 256, 256), bf16),
        pltpu.VMEM((512, 512), f32),
        pltpu.VMEM((512, 512), f32),
        pltpu.VMEM((4, 128, NPC), bf16),
        pltpu.VMEM((4, 128, NPC), bf16),
        pltpu.VMEM((64, LNP), f32),
        pltpu.SemaphoreType.DMA((copies,)),
        pltpu.SemaphoreType.DMA((copies,)),
    ]
    filter_scratch = [
        pltpu.VMEM((1, ENT), jnp.int32),
        pltpu.VMEM((2, FACE), jnp.int32),
        pltpu.VMEM((32, 128), f32),
        pltpu.VMEM((128, 32), f32),
        pltpu.VMEM((128, ENT), bf16),
        pltpu.VMEM((32, ENT), bf16),
        pltpu.VMEM((512, ENT), bf16),
        pltpu.VMEM((1, ENT), jnp.int32),
        pltpu.VMEM((1, ENT), jnp.int32),
        pltpu.VMEM((1, ENT), f32),
        pltpu.VMEM((128, ENT), bf16),
        pltpu.VMEM((128, SPEC), bf16),
        pltpu.VMEM((64, 2 * FACE), f32),
        pltpu.VMEM((64, ENT), f32),
        pltpu.VMEM((64, HALF), f32),
        pltpu.VMEM((2, 512, NPC), bf16),
        pltpu.VMEM((DEGREE, 2, 64, FACE), bf16),
        pltpu.VMEM((DEGREE, 2, 64, FACE), bf16),
        pltpu.SemaphoreType.DMA((DEGREE, 2)),
        pltpu.SemaphoreType.DMA((DEGREE, 2)),
    ]
    return pl.pallas_call(
        functools.partial(kernel, doms),
        out_shape=jax.ShapeDtypeStruct((64, LNP), bf16),
        in_specs=[smem, smem] + [vmem] * 5,
        out_specs=vmem,
        scratch_shapes=finish_scratch + filter_scratch,
        compiler_params=pltpu.CompilerParams(
            collective_id=0, has_side_effects=True, vmem_limit_bytes=58 << 20),
        name="subspace_step",
    )(filter_bounds, cell_scale, start_states, stiffness, potential, connectivity, shared_nodes)


def solution(mesh):
    in_specs = (P("st", "dom"), P(), P("dom"), P("dom"), P("dom", None), P("dom", None, None), P())
    return jax.shard_map(
        functools.partial(body, mesh.shape["dom"]), mesh=mesh, in_specs=in_specs, out_specs=P("st", "dom"),
        check_vma=False)
```

```python
import functools
import jax
import jax.numpy as jnp
from jax import lax
from jax.experimental import pallas as pl
from jax.experimental.pallas import tpu as pltpu
from jax.sharding import PartitionSpec as P

f32 = jnp.float32
bf16 = jnp.bfloat16
DEGREE = 3
CELLS = 8
NPC = 512
ENT = CELLS * NPC
LN = 3480
LNP = 3584
SH = 435
FACE = 512
SPEC = 1536
HALF = 2048
MESH_ID = pl.DeviceIdType.MESH


def one_hot_rows(row, count):
    ids = lax.broadcasted_iota(jnp.int32, (count, row.shape[1]), 0)
    return jnp.where(ids == row, 1.0, 0.0).astype(bf16)


def as_column(row):
    return jnp.transpose(jnp.broadcast_to(row, (128, 128)))


def contract_last(a, b):
    return lax.dot_general(a, b, (((1,), (1,)), ((), ())), preferred_element_type=f32)


def dot(a, b):
    return jnp.dot(a, b, preferred_element_type=f32)


def node_tables(faces, oa, ob):
    total = jnp.zeros((128, 32), f32)
    seen = []
    for c in range(CELLS):
        seen.append(total)
        part = slice(c * NPC, (c + 1) * NPC)
        total = total + contract_last(oa[:, part], ob[:, part])
    place = lax.broadcasted_iota(jnp.int32, (1, FACE), 1)
    face_tabs = []
    for side in range(2):
        row = faces[side : side + 1]
        fa = one_hot_rows(lax.shift_right_arithmetic(row, 5), 128)
        fb = one_hot_rows(lax.bitwise_and(row, 31), 32)
        high = (fa * lax.shift_right_logical(place, 7).astype(f32).astype(bf16)).astype(bf16)
        low = (fa * lax.bitwise_and(place, 127).astype(f32).astype(bf16)).astype(bf16)
        face_tabs.append((contract_last(fa, fb), contract_last(high, fb), contract_last(low, fb)))
    (is_l, l_hi, l_lo), (is_r, r_hi, r_lo) = face_tabs
    other = jnp.where((total > 1.5) & (is_l + is_r < 0.5), 1.0, 0.0)
    before_b = jnp.where(
        lax.broadcasted_iota(jnp.int32, (32, 32), 0) < lax.broadcasted_iota(jnp.int32, (32, 32), 1), 1.0, 0.0
    ).astype(bf16)
    before_a = jnp.where(
        lax.broadcasted_iota(jnp.int32, (128, 128), 1) < lax.broadcasted_iota(jnp.int32, (128, 128), 0), 1.0, 0.0
    ).astype(bf16)
    row_sum = jnp.broadcast_to(jnp.sum(other, axis=1, keepdims=True), (128, 32))
    rank = dot(other.astype(bf16), before_b) + dot(before_a, row_sum.astype(bf16))
    rank = rank.astype(jnp.int32)
    slot = rank + jnp.where(rank < FACE - SH, SH, 2 * SH)
    o_hi = lax.shift_right_logical(slot, 7).astype(f32)
    o_lo = lax.bitwise_and(slot, 127).astype(f32)
    hi = jnp.where(is_l > 0.5, l_hi, jnp.where(is_r > 0.5, r_hi + FACE // 128, jnp.where(other > 0.5, o_hi, -1.0)))
    lo = jnp.where(is_l > 0.5, l_lo, jnp.where(is_r > 0.5, r_lo, jnp.where(other > 0.5, o_lo, 0.0)))
    return hi, lo, total, seen


def at_entries(tables, oa, ob):
    stacked = jnp.concatenate(tables, axis=1).astype(bf16)
    picked = lax.dot_general(stacked, oa, (((0,), (0,)), ((), ())), preferred_element_type=f32)
    wide = ob.astype(f32)
    return [
        jnp.sum(picked[32 * k : 32 * (k + 1)] * wide, axis=0, keepdims=True) for k in range(len(tables))
    ]


def split(x):
    high = x.astype(bf16)
    return high, (x - high.astype(f32)).astype(bf16)


def filter_states(
    doms, wait_for_peers, bounds, scale, x_ref, stiff_ref, pot_ref, conn_ref, faces_ref,
    out_ref, weight_ref, first_ref,
    big, nodes, faces, pot_rows, pot_tab, oa, ob, hot, qa_ref, qb_ref, wpot_ref, parts, rows, sums, local, spread, field,
    send, recv, send_sem, recv_sem,
):
    d = lax.axis_index("dom")
    has_left = d > 0
    has_right = d < doms - 1
    for c in range(CELLS):
        nodes[:, c * NPC : (c + 1) * NPC] = conn_ref[c : c + 1]
    faces[...] = jnp.full((2, FACE), -1, jnp.int32)
    faces[:, 0:SH] = faces_ref[0]
    pot_rows[...] = jnp.zeros((32, 128), f32)
    for k in range(LNP // 128):
        pot_rows[k : k + 1] = pot_ref[pl.ds(k * 128, 128)].reshape(1, 128)
    for k in range(4):
        pot_tab[pl.ds(k, 32, stride=4)] = pot_rows[:, k * 32 : (k + 1) * 32]
    conn = nodes[...]
    oa[...] = one_hot_rows(lax.shift_right_logical(conn, 5), 128)
    ob[...] = one_hot_rows(lax.bitwise_and(conn, 31), 32)
    hi_tab, lo_tab, count, seen = node_tables(faces[...], oa, ob)
    pot = pot_tab[...]
    pot_hi = pot.astype(bf16).astype(f32)
    pot_mid = (pot - pot_hi).astype(bf16).astype(f32)
    pot_lo = pot - pot_hi - pot_mid
    for c in range(CELLS):
        part = slice(c * NPC, (c + 1) * NPC)
        qa, qb, cnt, p0, p1, p2, prior = at_entries(
            [hi_tab, lo_tab, count, pot_hi, pot_mid, pot_lo, seen[c]], oa[:, part], ob[:, part]
        )
        qa_ref[:, part] = qa.astype(jnp.int32)
        qb_ref[:, part] = qb.astype(jnp.int32)
        wpot_ref[:, part] = (p0 + p1 + p2) / cnt
        is_first = prior < 0.5
        on_left = (qa >= 0.0) & (qa * 128.0 + qb < SH) & has_left
        weight_ref[:, part] = jnp.where(is_first & jnp.logical_not(on_left), 1.0, 0.0)
        first_ref[:, part] = jnp.where(is_first, conn[:, part], -1)

    low_hot = one_hot_rows(lax.bitwise_and(conn, 127), 128)
    block = lax.shift_right_logical(conn, 7)
    chunk = 4
    for g in range(LNP // 128 // chunk):
        for k in range(chunk):
            mine = jnp.where(block == g * chunk + k, 1.0, 0.0).astype(bf16)
            hot[k * 128 : (k + 1) * 128] = low_hot * mine
        term = dot(x_ref[:, g * chunk * 128 : (g + 1) * chunk * 128], hot[...])
        local[...] = term if g == 0 else local[...] + term
    for c in range(CELLS):
        field[0, c * 64 : (c + 1) * 64] = local[:, c * NPC : (c + 1) * NPC].astype(bf16)

    qb_hot = one_hot_rows(qb_ref[...], 128)
    for j in range(SPEC // 128):
        mine = jnp.where(qa_ref[...] == j, 1.0, 0.0).astype(bf16)
        for h in range(2):
            big[h * SPEC + j * 128 : h * SPEC + (j + 1) * 128, SPEC:LNP] = (
                qb_hot[:, h * HALF : (h + 1) * HALF] * mine[:, h * HALF : (h + 1) * HALF])
    lane = lax.broadcasted_iota(jnp.int32, (128, 128), 1)

    @pl.loop(0, ENT // 128)
    def _(i):
        part = pl.ds(pl.multiple_of(i * 128, 128), 128)
        qa_col = as_column(qa_ref[:, part])
        qb_col = jnp.where(as_column(qb_ref[:, part]) == lane, 1.0, 0.0).astype(bf16)
        for j in range(SPEC // 128):
            mine = jnp.where(qa_col == j, 1.0, 0.0).astype(bf16)
            big[part, j * 128 : (j + 1) * 128] = qb_col * mine

    wait_for_peers()
    center = (bounds[1] + bounds[0]) / 2.0
    half_width = (bounds[1] - bounds[0]) / 2.0
    in_face = lax.broadcasted_iota(jnp.int32, (1, FACE), 1) < SH
    for step in range(DEGREE):
        old = field.at[(step + 1) % 2]
        now = field.at[step % 2]
        products = dot(now[...], stiff_ref[...])
        for c in range(CELLS):
            part = slice(c * NPC, (c + 1) * NPC)
            block_rows = slice(c * 64, (c + 1) * 64)
            value = products[block_rows] * scale[c] + wpot_ref[:, part] * now[block_rows].astype(f32)
            local[:, part] = value
            high, low = split(value)
            parts[0:64, part] = high
            parts[64:128, part] = low
        both = dot(parts[...], big[:, 0 : 2 * FACE])
        sums[:, 0 : 2 * FACE] = both[0:64] + both[64:128]
        send[step, 0] = sums[:, 0:FACE].astype(bf16)
        send[step, 1] = sums[:, FACE : 2 * FACE].astype(bf16)
        down = pltpu.make_async_remote_copy(
            src_ref=send.at[step, 0], dst_ref=recv.at[step, 1],
            send_sem=send_sem.at[step, 0], recv_sem=recv_sem.at[step, 1],
            device_id={"dom": d - 1}, device_id_type=MESH_ID)
        up = pltpu.make_async_remote_copy(
            src_ref=send.at[step, 1], dst_ref=recv.at[step, 0],
            send_sem=send_sem.at[step, 1], recv_sem=recv_sem.at[step, 0],
            device_id={"dom": d + 1}, device_id_type=MESH_ID)

        @pl.when(has_left)
        def _():
            down.start()

        @pl.when(has_right)
        def _():
            up.start()

        both = dot(parts[...], big[:, 2 * FACE : SPEC])
        high, low = split(both[0:64] + both[64:128])
        rows[0:64, 2 * FACE : SPEC] = high
        rows[64:128, 2 * FACE : SPEC] = low
        others = [
            dot(rows[:, 2 * FACE : SPEC], big[h * SPEC + 2 * FACE : (h + 1) * SPEC, SPEC:LNP]) for h in range(2)]

        @pl.when(has_left)
        def _():
            down.wait_send()
            up.wait_recv()

        @pl.when(has_right)
        def _():
            up.wait_send()
            down.wait_recv()

        for side, there in ((0, has_left), (1, has_right)):
            part = slice(side * FACE, (side + 1) * FACE)
            came = jnp.where(in_face & there, recv[step, side].astype(f32), 0.0)
            high, low = split(sums[:, part] + came)
            rows[0:64, part] = high
            rows[64:128, part] = low
        for h in range(2):
            both = others[h] + dot(rows[:, 0 : 2 * FACE], big[h * SPEC : h * SPEC + 2 * FACE, SPEC:LNP])
            spread[:, h * HALF : (h + 1) * HALF] = both[0:64] + both[64:128]
        for c in range(CELLS):
            part = slice(c * NPC, (c + 1) * NPC)
            block_rows = slice(c * 64, (c + 1) * 64)
            h = jnp.where(qa_ref[:, part] >= 0, spread[:, part], local[:, part])
            fresh = (h - center * now[block_rows].astype(f32)) / half_width
            if step > 0:
                fresh = 2.0 * fresh - old[block_rows].astype(f32)
            if step == DEGREE - 1:
                out_ref[block_rows] = fresh.astype(bf16)
            else:
                old[block_rows] = fresh.astype(bf16)


def product(a, b):
    a_hi, a_lo = split(a)
    b_hi, b_lo = split(b)
    return dot(a_hi, b_hi) + (dot(a_hi, b_lo) + dot(a_lo, b_hi))


def kernel(doms, bounds, scale, x_ref, stiff_ref, pot_ref, conn_ref, faces_ref, out_ref, *scratch):
    hot, mine_ref, weight_ref, first_ref = scratch[0:4]
    (got, sums, half, from_core, from_plane, line, total, gram, root, turned, back, acc, sent, came) = scratch[4:18]
    d = lax.axis_index("dom")
    s = lax.axis_index("st")
    core, y, z_lo = lax.rem(d, 2), lax.rem(lax.div(d, 2), 4), lax.div(d, 8)
    x, z_hi = lax.rem(s, 4), lax.div(s, 4)
    z = z_hi * 4 + z_lo

    def device(core=core, y=y, z_lo=z_lo, x=x, z_hi=z_hi):
        return {"dom": (z_lo * 4 + y) * 2 + core, "st": z_hi * 4 + x}

    def around(at, by, count):
        return lax.rem(at + by, count)

    def along_z(by):
        there = around(z, by, 8)
        return device(z_lo=lax.rem(there, 4), z_hi=lax.div(there, 4))

    count = [0]

    def copy(src, dst, to):
        k = count[0]
        count[0] += 1
        return pltpu.make_async_remote_copy(
            src_ref=src, dst_ref=dst, send_sem=sent.at[k], recv_sem=came.at[k], device_id=to, device_id_type=MESH_ID)

    def start(copies):
        for one in copies:
            one.start()
        return copies

    def finish(copies):
        for one in copies:
            one.wait()

    peers = [device(core=1 - core)]
    peers += [
        device(x=around(x, kx, 4), y=around(y, ky, 4)) for kx in range(4) for ky in range(4) if kx + ky]
    peers += [along_z(k) for k in range(1, 8)]
    peers += [device(x=around(x, k, 4), z_hi=1 - z_hi) for k in range(1, 4)]
    peers += [{"dom": lax.rem(d + 1, doms)}, {"dom": lax.rem(d + doms - 1, doms)}]
    barrier = pltpu.get_barrier_semaphore()
    for peer in peers:
        pl.semaphore_signal(barrier, inc=1, device_id=peer, device_id_type=MESH_ID)
    filter_states(
        doms, lambda: pl.semaphore_wait(barrier, len(peers)), bounds, scale, x_ref, stiff_ref, pot_ref, conn_ref,
        faces_ref, mine_ref, weight_ref, first_ref, hot, *scratch[18:])

    def pair_rows(at):
        return pl.ds(pl.multiple_of(at * 128, 128), 128)

    def cell_rows(at, k):
        return pl.ds(pl.multiple_of(at * 128 + k * 64, 64), 64)

    crossing = []
    for k in range(4):
        there = around(x, k, 4)
        crossing.append(copy(
            mine_ref.at[cell_rows(there, 1 - z_hi)], got.at[s, cell_rows(0, 1 - z_hi)],
            device(x=there, z_hi=1 - z_hi)))
    start(crossing)
    beside = []
    for k in range(1, 4):
        there = around(x, k, 4)
        beside.append(copy(mine_ref.at[pair_rows(there)], got.at[s], device(x=there)))
    start(beside)
    late = []
    for k in range(4):
        there = around(x, k, 4)
        late.append(copy(
            mine_ref.at[cell_rows(there, z_hi)], got.at[s, cell_rows(0, z_hi)],
            device(x=there, z_hi=1 - z_hi)))
    got[s] = mine_ref[pair_rows(x)]

    lane = lax.broadcasted_iota(jnp.int32, (128, 128), 1)

    @pl.loop(0, ENT // 128)
    def _(i):
        at = pl.ds(pl.multiple_of(i * 128, 128), 128)
        node = as_column(first_ref[:, at])
        low = jnp.where(lax.bitwise_and(node, 127) == lane, 1.0, 0.0).astype(bf16)
        block = lax.shift_right_arithmetic(node, 7)
        for j in range(LNP // 128):
            mine = jnp.where(block == j, 1.0, 0.0).astype(bf16)
            hot[at, j * 128 : (j + 1) * 128] = low * mine

    finish(beside)

    def weighted(rows, at):
        mark = weight_ref[:, pl.ds(pl.multiple_of(at * NPC, NPC), NPC)]
        return (rows.astype(f32) * mark).astype(bf16)

    own = pl.ds(pl.multiple_of(z_hi * 4, 4), 4)
    first_cell = got[own, 0:64].reshape(256, NPC)
    second_cell = got[own, 64:128].reshape(256, NPC)
    sums[0] = contract_last(weighted(first_cell, 2 * x), first_cell) + contract_last(
        weighted(second_cell, 2 * x + 1), second_cell)
    half[0] = sums[0].astype(bf16)
    finish(crossing)
    start(late[0:2])
    shared_rows = pl.ds(pl.multiple_of(z_hi * 64, 64), 64)
    low_half = got[0:4, shared_rows].reshape(256, NPC)
    high_half = got[4:8, shared_rows].reshape(256, NPC)
    sums[1] = contract_last(weighted(low_half, 2 * x + z_hi), high_half)

    half[1] = sums[1].astype(bf16)
    finish(start([copy(half.at[1 - core], from_core, device(core=1 - core))]))
    sums[core] = sums[core] + from_core[...].astype(f32)
    half[core] = sums[core].astype(bf16)
    plane = [(kx, ky) for kx in range(4) for ky in range(4)][1:]

    def piece_of(kx, ky):
        return pl.ds(pl.multiple_of(around(x, kx, 4) * 64 + around(y, ky, 4) * 16, 16), 16)

    def in_plane(kx, ky):
        return device(x=around(x, kx, 4), y=around(y, ky, 4))

    finish(start([
        copy(half.at[core, piece_of(*by)], from_plane.at[k], in_plane(*by)) for k, by in enumerate(plane)]))
    piece = sums[core, piece_of(0, 0)]
    for k in range(15):
        piece = piece + from_plane[k].astype(f32)
    line[z] = piece.astype(bf16)
    finish(start([copy(line.at[z], line.at[z], along_z(k)) for k in range(1, 8)]))
    start(late[2:4])
    low_sum = line[0].astype(f32)
    high_sum = line[4].astype(f32)
    for k in range(1, 4):
        low_sum = low_sum + line[k].astype(f32)
        high_sum = high_sum + line[4 + k].astype(f32)
    on_core = 2 * core
    piece_rows = piece_of(0, 0)

    @pl.when(core == 0)
    def _():
        total[1, piece_rows] = high_sum.astype(bf16)

    total[on_core, piece_rows] = (low_sum + jnp.where(core == 1, high_sum, 0.0)).astype(bf16)
    held = [copy(total.at[pl.ds(0, 2), piece_rows], total.at[pl.ds(0, 2), piece_rows], in_plane(*by)) for by in plane]
    count[0] -= len(plane)
    held_one = [copy(total.at[2, piece_rows], total.at[2, piece_rows], in_plane(*by)) for by in plane]

    came_from = [piece_rows] + [piece_of(4 - kx, 4 - ky) for kx, ky in plane]
    other_core = device(core=1 - core)
    passed = [copy(total.at[pl.ds(0, 2), at], total.at[pl.ds(0, 2), at], other_core) for at in came_from]
    count[0] -= len(came_from)
    passed_one = [copy(total.at[2, at], total.at[2, at], other_core) for at in came_from]

    def pass_on(arriving, onward, awaited):
        start(arriving)
        onward[0].start()
        for one, after in zip(arriving, onward[1:]):
            one.wait_recv()
            after.start()
        for one in arriving + onward:
            one.wait_send()
        for one in awaited:
            one.wait_recv()

    @pl.when(core == 0)
    def _():
        pass_on(held, passed, passed_one)

    @pl.when(core == 1)
    def _():
        pass_on(held_one, passed_one, passed)

    upper = total[2].astype(f32)
    gram[0:256, 0:256] = total[0].astype(f32)
    gram[256:512, 256:512] = total[1].astype(f32)
    gram[0:256, 256:512] = upper
    gram[256:512, 0:256] = jnp.transpose(upper)
    g = gram[...]
    frobenius = jnp.sqrt(jnp.sum(jnp.sum(g * g, axis=1, keepdims=True), axis=0, keepdims=True) + 1e-06)
    a = g / frobenius
    gram[...] = a
    square = product(a, a)
    diagonal = lax.broadcasted_iota(jnp.int32, (512, 512), 0) == lax.broadcasted_iota(jnp.int32, (512, 512), 1)
    root[...] = (
        jnp.where(diagonal, 2.25, 0.0) - 2.4375 * a + 1.6875 * square
        + product(square, 0.0625 * square - 0.5625 * a))
    columns = root[:, pl.ds(pl.multiple_of(z_hi * 256, 256), 256)]
    cubed = product(root[...], product(root[...], columns))
    coeffs = ((1.5 * columns - 0.5 * product(gram[...], cubed)) / jnp.sqrt(frobenius)).astype(bf16)

    finish(late)
    for k in range(2):
        cell = got[:, k * 64 : (k + 1) * 64].reshape(512, NPC)
        rotated = lax.dot_general(coeffs, cell, (((0,), (0,)), ((), ())), preferred_element_type=f32)
        turned[:, k * 64 : (k + 1) * 64] = rotated.astype(bf16).reshape(4, 64, NPC)
    returned = start([
        copy(turned.at[around(x, k, 4)], back.at[x], device(x=around(x, k, 4))) for k in range(1, 4)])
    back[x] = turned[x]
    for k in range(4):
        source = around(x, 4 - k, 4)
        if k:
            returned[k - 1].wait()
        pair = jnp.concatenate([back[source, 0:64], back[source, 64:128]], axis=1)
        term = dot(pair, hot[pl.ds(pl.multiple_of(source * 1024, 1024), 1024)])
        if k == 0:
            acc[...] = term
        elif k < 3:
            acc[...] = acc[...] + term
        else:
            out_ref[...] = (acc[...] + term).astype(bf16)


def body(doms, start_states, stiffness, cell_scale, potential, connectivity, shared_nodes, filter_bounds):
    vmem = pl.BlockSpec(memory_space=pltpu.VMEM)
    smem = pl.BlockSpec(memory_space=pltpu.SMEM)
    copies = 11 + 1 + 15 + 7 + 15 + 16 + 3
    finish_scratch = [
        pltpu.VMEM((ENT, LNP), bf16),
        pltpu.VMEM((512, NPC), bf16),
        pltpu.VMEM((1, ENT), f32),
        pltpu.VMEM((1, ENT), jnp.int32),
        pltpu.VMEM((8, 128, NPC), bf16),
        pltpu.VMEM((2, 256, 256), f32),
        pltpu.VMEM((2, 256, 256), bf16),
        pltpu.VMEM((256, 256), bf16),
        pltpu.VMEM((15, 16, 256), bf16),
        pltpu.VMEM((8, 16, 256), bf16),
        pltpu.VMEM((3, 256, 256), bf16),
        pltpu.VMEM((512, 512), f32),
        pltpu.VMEM((512, 512), f32),
        pltpu.VMEM((4, 128, NPC), bf16),
        pltpu.VMEM((4, 128, NPC), bf16),
        pltpu.VMEM((64, LNP), f32),
        pltpu.SemaphoreType.DMA((copies,)),
        pltpu.SemaphoreType.DMA((copies,)),
    ]
    filter_scratch = [
        pltpu.VMEM((1, ENT), jnp.int32),
        pltpu.VMEM((2, FACE), jnp.int32),
        pltpu.VMEM((32, 128), f32),
        pltpu.VMEM((128, 32), f32),
        pltpu.VMEM((128, ENT), bf16),
        pltpu.VMEM((32, ENT), bf16),
        pltpu.VMEM((512, ENT), bf16),
        pltpu.VMEM((1, ENT), jnp.int32),
        pltpu.VMEM((1, ENT), jnp.int32),
        pltpu.VMEM((1, ENT), f32),
        pltpu.VMEM((128, ENT), bf16),
        pltpu.VMEM((128, SPEC), bf16),
        pltpu.VMEM((64, 2 * FACE), f32),
        pltpu.VMEM((64, ENT), f32),
        pltpu.VMEM((64, ENT), f32),
        pltpu.VMEM((2, 512, NPC), bf16),
        pltpu.VMEM((DEGREE, 2, 64, FACE), bf16),
        pltpu.VMEM((DEGREE, 2, 64, FACE), bf16),
        pltpu.SemaphoreType.DMA((DEGREE, 2)),
        pltpu.SemaphoreType.DMA((DEGREE, 2)),
    ]
    return pl.pallas_call(
        functools.partial(kernel, doms),
        out_shape=jax.ShapeDtypeStruct((64, LNP), bf16),
        in_specs=[smem, smem] + [vmem] * 5,
        out_specs=vmem,
        scratch_shapes=finish_scratch + filter_scratch,
        compiler_params=pltpu.CompilerParams(
            collective_id=0, has_side_effects=True, vmem_limit_bytes=58 << 20),
        name="subspace_step",
    )(filter_bounds, cell_scale, start_states, stiffness, potential, connectivity, shared_nodes)


def solution(mesh):
    in_specs = (P("st", "dom"), P(), P("dom"), P("dom"), P("dom", None), P("dom", None, None), P())
    return jax.shard_map(
        functools.partial(body, mesh.shape["dom"]), mesh=mesh, in_specs=in_specs, out_specs=P("st", "dom"),
        check_vma=False)
```
